256 devices in a mesh: seq: 32 (over y, z), head: 8 (over x, core).
Axes of the slice: x: 4, y: 4, z: 8, core: 2. Of those that a mesh axis runs over, the one named last changes fastest.
Arguments:
- queries: bfloat16 [16384, 8192], P('seq', 'head'), may hold values from -4 to 4
- key_vecs: bfloat16 [16384, 8192], P('seq', 'head'), may hold values from -4 to 4
- value_vecs: bfloat16 [16384, 8192], P('seq', 'head'), may hold values from -6 to 6
- log_decay: float32 [16384, 64], P('seq', 'head'), may hold values from -3 to 0, as said below
- norm_gain: float32 [8192], P('head'), may hold values from 0.1 to 1.9
- cotangent: bfloat16 [16384, 8192], P('seq', 'head'), may hold values from -6 to 6
Outputs:
- attended: bfloat16 [16384, 8192], P('seq', 'head')
- grad_queries: bfloat16 [16384, 8192], P('seq', 'head')
- grad_keys: bfloat16 [16384, 8192], P('seq', 'head')
- grad_values: bfloat16 [16384, 8192], P('seq', 'head')
The draws below stay inside these ranges and needn't reach their ends.
Inputs may be any that keep to these rules, and one draw needn't show every extreme that they name: `log_decay`: every entry is negative.
All inputs are finite; a program needn't handle non-finite values.
Results may differ from the reference program's by a relative error of at most 0.0051.
Values sent between devices are 32-bit elements; how exact they have to be, the bound alone decides.
A program may use at most 128 MiB of HBM per device.

```python
import math
import jax
import jax.numpy as jnp
from jax import lax

HEAD_TOTAL = 64
HEAD_DIM = 128
TOK_DEV = 512
BLOCK = 512
SEQUENCE_LENGTH = 16384


def draw_log_decay(key, part):
    every_key = jax.random.split(key, 7)
    fast_share = 0.5
    is_fast = jax.random.bernoulli(every_key[0], fast_share, (HEAD_TOTAL,))
    fast_rate = jnp.exp(jax.random.uniform(every_key[1], (HEAD_TOTAL,), jnp.float32, math.log(0.04), math.log(0.08)))
    slow_rate = jnp.exp(jax.random.uniform(every_key[2], (HEAD_TOTAL,), jnp.float32, math.log(0.1), math.log(0.5)))
    slow_rate = slow_rate * (math.log(10.0) / SEQUENCE_LENGTH)
    shard_count = SEQUENCE_LENGTH // TOK_DEV
    is_hard = jax.random.bernoulli(every_key[6], 1.0 / 3.0, (shard_count, HEAD_TOTAL))
    positions = jnp.arange(SEQUENCE_LENGTH)
    shard_of = positions // TOK_DEV
    within = positions % BLOCK
    rim_width = 3 * BLOCK // 16
    middle = (within >= rim_width) & (within < BLOCK - rim_width)
    hard_rows = is_hard[shard_of]
    fast_here = is_fast[None, :] & hard_rows & middle[:, None]
    baseline_rate = jnp.where(fast_here, fast_rate[None, :], slow_rate[None, :])
    jitter_level = jax.random.uniform(every_key[3], (SEQUENCE_LENGTH, HEAD_TOTAL), jnp.float32, 0.5, 1.5)
    spike_positions = jax.random.randint(every_key[4], (4,), 0, SEQUENCE_LENGTH)
    spike_depth = jax.random.uniform(every_key[5], (4, HEAD_TOTAL), jnp.float32, math.log(0.5), math.log(0.8))
    spike_flags = (positions[:, None] == spike_positions[None, :]).astype(jnp.float32)
    return -baseline_rate * jitter_level + spike_flags @ spike_depth


def level_of(stream_key, shape, pieces, low, largest):
    def one(dim, parts):
        steps = jax.random.uniform(jax.random.fold_in(jax.random.fold_in(stream_key, 6), dim), (parts,), jnp.float32, low / len(pieces), largest / len(pieces))
        return jnp.repeat(jnp.exp(steps), shape[dim] // parts).reshape((-1,) + (1,) * (len(shape) - dim - 1))

    gain = one(*pieces[0])
    for cut in pieces[1:]:
        gain = gain * one(*cut)
    return gain


def noise(rng, extent, scale, bound, cuts=(), held_as=jnp.bfloat16):
    level = level_of(rng, extent, cuts, -0.22, 0.18) if cuts else 1.0
    result = jax.random.normal(rng, extent, jnp.float32) * scale * level
    return jnp.minimum(jnp.maximum(result, -bound), bound).astype(held_as)


def setup_inputs(seed: int = 0) -> dict:
    splits = jax.random.split(jax.random.key(seed), 7)
    queries = noise(splits[0], (SEQUENCE_LENGTH, HEAD_TOTAL * HEAD_DIM), 0.3, 4.0, ((0, 32), (1, 8)))
    key_vecs = noise(splits[1], (SEQUENCE_LENGTH, HEAD_TOTAL * HEAD_DIM), 0.3, 4.0, ((0, 32), (1, 8)))
    value_vecs = noise(splits[2], (SEQUENCE_LENGTH, HEAD_TOTAL * HEAD_DIM), 1.0, 6.0, ((0, 32), (1, 8)))
    log_decay = draw_log_decay(jax.random.fold_in(splits[6], 71), 0)
    norm_gain = jnp.clip(1.0 + 0.18 * jax.random.normal(splits[4], (HEAD_TOTAL * HEAD_DIM,), jnp.float32), 0.1, 1.9)
    cotangent = noise(splits[5], (SEQUENCE_LENGTH, HEAD_TOTAL * HEAD_DIM), 1.0, 6.0, ((0, 32), (1, 8)))
    return {"queries": queries, "key_vecs": key_vecs, "value_vecs": value_vecs, "log_decay": log_decay, "norm_gain": norm_gain, "cotangent": cotangent}


highest = lax.Precision.HIGHEST
epsilon = 1e-06

def as_float(array):
    return array.astype(jnp.float32)

def block_decay(cumulative):
    transposed = cumulative.T
    spread_log = transposed[:, :, None] - transposed[:, None, :]
    length = cumulative.shape[0]
    causal = (jnp.arange(length)[:, None] >= jnp.arange(length)[None, :])[None]
    return jnp.where(causal, jnp.exp(jnp.where(causal, spread_log, 0.0)), 0.0)

def reference(queries, key_vecs, value_vecs, log_decay, norm_gain, cotangent):
    block_count = SEQUENCE_LENGTH // BLOCK
    feature_count = HEAD_TOTAL * HEAD_DIM

    def to_blocks(array):
        return array.reshape(block_count, BLOCK, HEAD_TOTAL, HEAD_DIM)
    query_blocks = to_blocks(queries)
    key_blocks = to_blocks(key_vecs)
    value_blocks = to_blocks(value_vecs)
    cumulative = jnp.cumsum(log_decay.reshape(block_count, BLOCK, HEAD_TOTAL), axis=1)
    totals = cumulative[:, -1, :]
    zero_state = jnp.zeros((HEAD_TOTAL, HEAD_DIM, HEAD_DIM), jnp.float32)

    def forward_step(running, inputs):
        query_block, key_block, value_block, block_cumul = inputs
        decays = block_decay(block_cumul)
        scores = jnp.einsum('thd,shd->hts', as_float(query_block), as_float(key_block))
        weights = (scores * decays).astype(jnp.bfloat16)
        inner_out = jnp.einsum('hts,shd->thd', as_float(weights), as_float(value_block))
        outer_out = jnp.exp(block_cumul)[:, :, None] * jnp.einsum('thd,hde->the', as_float(query_block), running, precision=highest)
        scaled_keys = as_float(key_block) * jnp.exp(block_cumul[-1][None] - block_cumul)[:, :, None]
        block_piece = jnp.einsum('shd,she->hde', scaled_keys, as_float(value_block), precision=highest)
        advanced = jnp.exp(block_cumul[-1])[:, None, None] * running + block_piece
        return (advanced, (inner_out + outer_out, running))
    final_state, (outputs, before) = lax.scan(forward_step, zero_state, (query_blocks, key_blocks, value_blocks, cumulative))
    flat_out = outputs.reshape(SEQUENCE_LENGTH, feature_count)
    inverse = lax.rsqrt(lax.optimization_barrier(jnp.sum(flat_out * flat_out, axis=1)) / feature_count + epsilon)
    normed = flat_out * inverse[:, None]
    attended = (normed * norm_gain[None]).astype(jnp.bfloat16)
    scaled_grad = as_float(cotangent) * norm_gain[None]
    mean_term = inverse * lax.optimization_barrier(jnp.sum(scaled_grad * flat_out, axis=1)) / feature_count
    grad_out = (inverse[:, None] * (scaled_grad - normed * mean_term[:, None])).astype(jnp.bfloat16)
    grad_blocks = to_blocks(grad_out)

    def backward_inner(inputs):
        query_block, key_block, value_block, block_cumul, grad_block = inputs
        decays = block_decay(block_cumul)
        scores = jnp.einsum('thd,shd->hts', as_float(query_block), as_float(key_block))
        weights = (scores * decays).astype(jnp.bfloat16)
        grad_scores = jnp.einsum('thd,shd->hts', as_float(grad_block), as_float(value_block))
        grad_weights = (grad_scores * decays).astype(jnp.bfloat16)
        inner_query = jnp.einsum('hts,shd->thd', as_float(grad_weights), as_float(key_block))
        inner_key = jnp.einsum('hts,thd->shd', as_float(grad_weights), as_float(query_block))
        inner_value = jnp.einsum('hts,thd->shd', as_float(weights), as_float(grad_block))
        lead_scale = jnp.exp(block_cumul)[:, :, None]
        grad_piece = jnp.einsum('thd,the->hde', as_float(query_block) * lead_scale, as_float(grad_block), precision=highest)
        return (inner_query, inner_key, inner_value, grad_piece)
    inner_query, inner_key, inner_value, grad_pieces = lax.map(backward_inner, (query_blocks, key_blocks, value_blocks, cumulative, grad_blocks))

    def backward_step(running, inputs):
        grad_piece, block_total = inputs
        return (grad_piece + jnp.exp(block_total)[:, None, None] * running, running)
    start_grad, after_grad = lax.scan(backward_step, zero_state, (grad_pieces, totals), reverse=True)
    lead_scale = jnp.exp(cumulative)[..., None]
    trail_scale = jnp.exp(totals[:, None, :] - cumulative)[..., None]
    grad_queries = inner_query + lead_scale * jnp.einsum('bthe,bhde->bthd', as_float(grad_blocks), before, precision=highest)
    grad_keys = inner_key + trail_scale * jnp.einsum('bshe,bhde->bshd', as_float(value_blocks), after_grad, precision=highest)
    grad_values = inner_value + trail_scale * jnp.einsum('bshd,bhde->bshe', as_float(key_blocks), after_grad, precision=highest)
    return (attended, grad_queries.reshape(SEQUENCE_LENGTH, feature_count).astype(jnp.bfloat16), grad_keys.reshape(SEQUENCE_LENGTH, feature_count).astype(jnp.bfloat16), grad_values.reshape(SEQUENCE_LENGTH, feature_count).astype(jnp.bfloat16))
```

```python
import functools

import jax
import jax.numpy as jnp
from jax import lax
from jax.experimental import pallas as pl
from jax.experimental.pallas import tpu as pltpu
from jax.sharding import PartitionSpec as P

DIM = 128
BLOCK = 512
HALF = 256
EPSILON = 1e-06
F32 = jnp.float32
BF16 = jnp.bfloat16
NN = (((1,), (0,)), ((), ()))
NT = (((1,), (1,)), ((), ()))
TN = (((0,), (0,)), ((), ()))


def mul(a, b, dims):
    return lax.dot_general(a, b, dims, preferred_element_type=F32)


def split(x):
    high = x.astype(BF16)
    return high, (x - high.astype(F32)).astype(BF16)


def kernel(
    seq_count, head_count, heads,
    log_ref, gain_ref, query_hbm, key_hbm, value_hbm, cot_hbm,
    att_hbm, gq_hbm, gk_hbm, gv_hbm,
    query, key, value, cot, att, gq, gk, gv,
    cum_row, cum_col, decay0, decay1, weight0, weight1,
    out, grad, inner_key, inner_value,
    own_total, totals,
    piece, arrived, before, state,
    grad_piece, grad_arrived, after, after_state,
    stat, stats,
    in_sem, out_sem, total_sem, first_sem, second_sem, stat_sem, third_sem, fourth_sem,
):
    me = lax.axis_index("seq")
    place = lax.axis_index("head")
    rows = piece.shape[1]
    parts = DIM // rows
    features = head_count * heads * DIM

    loads = [
        pltpu.make_async_copy(source, target, in_sem.at[i])
        for i, (source, target) in enumerate(
            ((key_hbm, key), (value_hbm, value), (query_hbm, query), (cot_hbm, cot))
        )
    ]
    for load in loads:
        load.start()

    barrier = pltpu.get_barrier_semaphore()

    def greet_seq(d, carry):
        pl.semaphore_signal(
            barrier, inc=1, device_id={"seq": lax.rem(me + d, seq_count)},
            device_id_type=pl.DeviceIdType.MESH,
        )
        return carry

    def greet_head(d, carry):
        pl.semaphore_signal(
            barrier, inc=1, device_id={"head": lax.rem(place + d, head_count)},
            device_id_type=pl.DeviceIdType.MESH,
        )
        return carry

    lax.fori_loop(1, seq_count, greet_seq, 0)
    lax.fori_loop(1, head_count, greet_head, 0)

    def columns(h):
        return pl.ds(pl.multiple_of(h * DIM, DIM), DIM)

    def exchange(source, target, send, receive, axis, mine, count, same):
        own = source if same else source.at[mine]
        pltpu.make_async_copy(own, target.at[mine], receive).start()

        def one(d, carry):
            peer = lax.rem(mine + d, count)
            pltpu.make_async_remote_copy(
                src_ref=source if same else source.at[peer],
                dst_ref=target.at[mine],
                send_sem=send,
                recv_sem=receive,
                device_id={axis: peer},
                device_id_type=pl.DeviceIdType.MESH,
            ).start()
            return carry

        lax.fori_loop(1, count, one, 0)

    def arrive(target, receive):
        pltpu.make_async_copy(target, target, receive).wait()

    def sent(target, send, count):
        some = target.at[pl.ds(0, count - 1)]
        pltpu.make_async_copy(some, some, send).wait()

    lower = lax.broadcasted_iota(jnp.int32, (BLOCK, BLOCK), 0) >= lax.broadcasted_iota(
        jnp.int32, (BLOCK, BLOCK), 1
    )
    cumulative = lax.dot_general(
        log_ref[...], lower.astype(F32), NT,
        precision=lax.Precision.HIGHEST, preferred_element_type=F32,
    )
    cum_row[...] = cumulative
    turned = jnp.transpose(jnp.concatenate([cumulative] * (DIM // heads), axis=0))
    for h in range(heads):
        spread = jnp.broadcast_to(turned[:, h : h + 1], (BLOCK, DIM))
        cum_col[:, h * DIM : (h + 1) * DIM] = spread
        for part in range(parts):
            own_total[part * heads + h] = spread[BLOCK - 1 :, :]

    pl.semaphore_wait(barrier, seq_count + head_count - 2)
    exchange(own_total, totals, total_sem.at[0], total_sem.at[1], "seq", me, seq_count, False)

    loads[0].wait()
    loads[1].wait()

    def store_piece(target, h, result):
        for part in range(parts):
            target[part * heads + h] = result[part * rows : (part + 1) * rows]

    def load_state(source, h):
        return jnp.concatenate([source[part * heads + h] for part in range(parts)], axis=0)

    def make_piece(h, carry):
        at = columns(h)
        cum = cum_col[:, at]
        trail = jnp.exp(own_total[h] - cum)
        high, low = split(key[:, at].astype(F32) * trail)
        both = value[:, at]
        store_piece(piece, h, mul(high, both, TN) + mul(low, both, TN))
        return carry

    lax.fori_loop(0, heads, make_piece, 0)
    exchange(piece, arrived, first_sem.at[0], first_sem.at[1], "seq", me, seq_count, False)

    loads[2].wait()
    loads[3].wait()
    causal = lax.broadcasted_iota(jnp.int32, (HALF, HALF), 0) >= lax.broadcasted_iota(
        jnp.int32, (HALF, HALF), 1
    )

    def forward(h, carry):
        at = columns(h)
        row = cum_row[pl.ds(h, 1), :]
        top = cum_col[:HALF, at]
        top = jnp.concatenate([top, top], axis=1)
        low = cum_col[HALF:, at]
        low = jnp.concatenate([low, low], axis=1)
        left, right = row[:, :HALF], row[:, HALF:]
        masked = -1e30
        d0 = jnp.exp(jnp.where(causal, top - left, masked))
        d1 = jnp.concatenate(
            [jnp.exp(low - left), jnp.exp(jnp.where(causal, low - right, masked))], axis=1
        )
        decay0[h] = d0
        decay1[h] = d1
        keys = key[:, at]
        values = value[:, at]
        w0 = (mul(query[:HALF, at], keys[:HALF], NT) * d0).astype(BF16)
        w1 = (mul(query[HALF:, at], keys, NT) * d1).astype(BF16)
        weight0[h] = w0
        weight1[h] = w1
        out[:HALF, at] = mul(w0, values[:HALF], NN)
        out[HALF:, at] = mul(w1, values, NN)
        return carry

    lax.fori_loop(0, heads, forward, 0)

    arrive(totals, total_sem.at[1])
    arrive(arrived, first_sem.at[1])

    def advance(b, running):
        before[b] = running
        return jnp.exp(totals[b]) * running + arrived[b]

    lax.fori_loop(0, seq_count, advance, jnp.zeros((rows, DIM), F32))
    exchange(before, state, second_sem.at[0], second_sem.at[1], "seq", me, seq_count, False)
    arrive(state, second_sem.at[1])

    def finish_out(h, carry):
        squares, inners = carry
        at = columns(h)
        lead = jnp.exp(cum_col[:, at])
        high, low = split(load_state(state, h))
        outer = mul(query[:, at], jnp.concatenate([high, low], axis=1), NN)
        whole = out[:, at] + lead * (outer[:, :DIM] + outer[:, DIM:])
        out[:, at] = whole
        scaled = cot[:, at].astype(F32) * gain_ref[:, at]
        return squares + whole * whole, inners + scaled * whole

    zero = jnp.zeros((BLOCK, DIM), F32)
    squares, inners = lax.fori_loop(0, heads, finish_out, (zero, zero))
    square_row = jnp.sum(jnp.transpose(squares), axis=0, keepdims=True)
    inner_row = jnp.sum(jnp.transpose(inners), axis=0, keepdims=True)
    for i in range(BLOCK // DIM):
        stat[i : i + 1, :] = square_row[:, i * DIM : (i + 1) * DIM]
        stat[4 + i : 5 + i, :] = inner_row[:, i * DIM : (i + 1) * DIM]
    exchange(stat, stats, stat_sem.at[0], stat_sem.at[1], "head", place, head_count, True)
    arrive(stats, stat_sem.at[1])
    summed = stats[0]
    for i in range(1, head_count):
        summed = summed + stats[i]
    inverse_rows = lax.rsqrt(summed[:4] / features + EPSILON)
    mean_rows = inverse_rows * summed[4:] / features

    def to_columns(four):
        return jnp.concatenate(
            [jnp.transpose(jnp.broadcast_to(four[i : i + 1], (DIM, DIM))) for i in range(4)], axis=0
        )

    inverse = to_columns(inverse_rows)
    mean_term = to_columns(mean_rows)

    def make_grad(h, carry):
        at = columns(h)
        gain = gain_ref[:, at]
        normed = out[:, at] * inverse
        att[:, at] = (normed * gain).astype(BF16)
        scaled = cot[:, at].astype(F32) * gain
        g = (inverse * (scaled - normed * mean_term)).astype(BF16)
        grad[:, at] = g
        high, low = split(query[:, at].astype(F32) * jnp.exp(cum_col[:, at]))
        store_piece(grad_piece, h, mul(high, g, TN) + mul(low, g, TN))
        return carry

    lax.fori_loop(0, heads, make_grad, 0)
    exchange(grad_piece, grad_arrived, third_sem.at[0], third_sem.at[1], "seq", me, seq_count, False)
    store_att = pltpu.make_async_copy(att, att_hbm, out_sem.at[0])
    store_att.start()

    def backward(h, carry):
        at = columns(h)
        d0 = decay0[h]
        d1 = decay1[h]
        keys = key[:, at]
        values = value[:, at]
        g = grad[:, at]
        q = query[:, at]
        w0 = weight0[h]
        w1 = weight1[h]
        g0 = (mul(g[:HALF], values[:HALF], NT) * d0).astype(BF16)
        g1 = (mul(g[HALF:], values, NT) * d1).astype(BF16)
        high, low = split(load_state(state, h))
        outer = mul(g, high, NT) + mul(g, low, NT)
        lead = jnp.exp(cum_col[:, at])
        gq[:HALF, at] = (mul(g0, keys[:HALF], NN) + lead[:HALF] * outer[:HALF]).astype(BF16)
        gq[HALF:, at] = (mul(g1, keys, NN) + lead[HALF:] * outer[HALF:]).astype(BF16)
        full_key = mul(g1, q[HALF:], TN)
        full_value = mul(w1, g[HALF:], TN)
        inner_key[:HALF, at] = full_key[:HALF] + mul(g0, q[:HALF], TN)
        inner_key[HALF:, at] = full_key[HALF:]
        inner_value[:HALF, at] = full_value[:HALF] + mul(w0, g[:HALF], TN)
        inner_value[HALF:, at] = full_value[HALF:]
        return carry

    lax.fori_loop(0, heads, backward, 0)
    store_gq = pltpu.make_async_copy(gq, gq_hbm, out_sem.at[1])
    store_gq.start()
    arrive(grad_arrived, third_sem.at[1])

    def retreat(turn, running):
        b = seq_count - 1 - turn
        after[b] = running
        return grad_arrived[b] + jnp.exp(totals[b]) * running

    lax.fori_loop(0, seq_count, retreat, jnp.zeros((rows, DIM), F32))
    exchange(after, after_state, fourth_sem.at[0], fourth_sem.at[1], "seq", me, seq_count, False)
    arrive(after_state, fourth_sem.at[1])

    def finish(h, carry):
        at = columns(h)
        high, low = split(load_state(after_state, h))
        trail = jnp.exp(own_total[h] - cum_col[:, at])
        values = value[:, at]
        from_value = mul(values, high, NT) + mul(values, low, NT)
        gk[:, at] = (inner_key[:, at] + trail * from_value).astype(BF16)
        from_key = mul(key[:, at], jnp.concatenate([high, low], axis=1), NN)
        gv[:, at] = (
            inner_value[:, at] + trail * (from_key[:, :DIM] + from_key[:, DIM:])
        ).astype(BF16)
        return carry

    lax.fori_loop(0, heads, finish, 0)
    store_gk = pltpu.make_async_copy(gk, gk_hbm, out_sem.at[2])
    store_gv = pltpu.make_async_copy(gv, gv_hbm, out_sem.at[3])
    store_gk.start()
    store_gv.start()

    sent(totals, total_sem.at[0], seq_count)
    sent(arrived, first_sem.at[0], seq_count)
    sent(state, second_sem.at[0], seq_count)
    sent(stats, stat_sem.at[0], head_count)
    sent(grad_arrived, third_sem.at[0], seq_count)
    sent(after_state, fourth_sem.at[0], seq_count)
    store_att.wait()
    store_gq.wait()
    store_gk.wait()
    store_gv.wait()


def on_device(seq_count, head_count, queries, key_vecs, value_vecs, log_decay, norm_gain, cotangent):
    tokens, width = queries.shape
    heads = width // DIM
    rows = heads * DIM // seq_count
    big = jax.ShapeDtypeStruct((tokens, width), BF16)
    vmem = pl.BlockSpec(memory_space=pltpu.VMEM)
    hbm = pl.BlockSpec(memory_space=pl.ANY)
    narrow = pltpu.VMEM((tokens, width), BF16)
    wide = pltpu.VMEM((tokens, width), F32)
    chunk = pltpu.VMEM((seq_count, rows, DIM), F32)
    line = pltpu.VMEM((seq_count, 1, DIM), F32)
    pair = pltpu.SemaphoreType.DMA((2,))
    four = pltpu.SemaphoreType.DMA((4,))
    return pl.pallas_call(
        functools.partial(kernel, seq_count, head_count, heads),
        out_shape=(big,) * 4,
        in_specs=[vmem, vmem] + [hbm] * 4,
        out_specs=(hbm,) * 4,
        scratch_shapes=[narrow] * 8
        + [
            pltpu.VMEM((heads, tokens), F32),
            wide,
            pltpu.VMEM((heads, HALF, HALF), F32),
            pltpu.VMEM((heads, HALF, BLOCK), F32),
            pltpu.VMEM((heads, HALF, HALF), BF16),
            pltpu.VMEM((heads, HALF, BLOCK), BF16),
            wide,
            narrow,
            wide,
            wide,
            line,
            line,
        ]
        + [chunk] * 8
        + [pltpu.VMEM((8, DIM), F32), pltpu.VMEM((head_count, 8, DIM), F32)]
        + [four, four]
        + [pair] * 6,
        compiler_params=pltpu.CompilerParams(
            collective_id=0, has_side_effects=True, vmem_limit_bytes=60 * 1024 * 1024
        ),
    )(log_decay.T, norm_gain.reshape(1, width), queries, key_vecs, value_vecs, cotangent)


def solution(mesh):
    return jax.shard_map(
        functools.partial(on_device, mesh.shape["seq"], mesh.shape["head"]),
        mesh=mesh,
        in_specs=(
            P("seq", "head"),
            P("seq", "head"),
            P("seq", "head"),
            P("seq", "head"),
            P("head"),
            P("seq", "head"),
        ),
        out_specs=(P("seq", "head"), P("seq", "head"), P("seq", "head"), P("seq", "head")),
        check_vma=False,
    )
```

```python
import functools

import jax
import jax.numpy as jnp
from jax import lax
from jax.experimental import pallas as pl
from jax.experimental.pallas import tpu as pltpu
from jax.sharding import PartitionSpec as P

DIM = 128
BLOCK = 512
HALF = 256
EPSILON = 1e-06
F32 = jnp.float32
BF16 = jnp.bfloat16
NN = (((1,), (0,)), ((), ()))
NT = (((1,), (1,)), ((), ()))
TN = (((0,), (0,)), ((), ()))


def mul(a, b, dims):
    return lax.dot_general(a, b, dims, preferred_element_type=F32)


def split(x):
    high = x.astype(BF16)
    return high, (x - high.astype(F32)).astype(BF16)


def store_kernel(*refs):
    sources, targets, sem = refs[:4], refs[4:8], refs[8]
    copies = [
        pltpu.make_async_copy(source, target, sem.at[i])
        for i, (source, target) in enumerate(zip(sources, targets))
    ]
    for copy in copies:
        copy.start()
    for copy in copies:
        copy.wait()


def kernel(
    planes, plane_size, head_count, heads, early, early_back,
    log_ref, gain_ref, query_hbm, key_hbm, value_hbm, cot_hbm,
    att, gq, gk, gv,
    query, key, value, cot,
    cum_row, cum_col, lead, trail, decay0, decay1, weight0, weight1,
    out, scaled, query_high, query_low, grad, inner_key, inner_value,
    own_total, totals,
    piece, arrived, before, state,
    grad_piece, grad_arrived, after, after_state,
    stat, stats,
    in_sem, total_sem, stat_sem, give_send, give_receive, take_send, take_receive,
):
    me = lax.axis_index("seq")
    plane = me // plane_size
    spot = lax.rem(me, plane_size)
    place = lax.axis_index("head")
    seq_count = planes * plane_size
    rows = piece.shape[1]
    half_rows = rows // 2
    features = head_count * heads * DIM

    loads = [
        pltpu.make_async_copy(source, target, in_sem.at[i])
        for i, (source, target) in enumerate(
            ((key_hbm, key), (value_hbm, value), (query_hbm, query), (cot_hbm, cot))
        )
    ]
    for load in loads:
        load.start()

    barrier = pltpu.get_barrier_semaphore()

    def greet_seq(d, carry):
        pl.semaphore_signal(
            barrier, inc=1, device_id={"seq": lax.rem(me + d, seq_count)},
            device_id_type=pl.DeviceIdType.MESH,
        )
        return carry

    def greet_head(d, carry):
        pl.semaphore_signal(
            barrier, inc=1, device_id={"head": lax.rem(place + d, head_count)},
            device_id_type=pl.DeviceIdType.MESH,
        )
        return carry

    lax.fori_loop(1, seq_count, greet_seq, 0)
    lax.fori_loop(1, head_count, greet_head, 0)

    def columns(h):
        return pl.ds(pl.multiple_of(h * DIM, DIM), DIM)

    def turn_of(i):
        return plane_size // 2 + (1 - 2 * lax.rem(i, 2)) * ((i + 1) // 2)

    def part_rows(part):
        return pl.ds(part * half_rows, half_rows)

    def slots(h):
        return pl.ds(pl.multiple_of(h * planes, planes), planes)

    def remote(source, target, send, receive, peer):
        pltpu.make_async_remote_copy(
            src_ref=source, dst_ref=target, send_sem=send, recv_sem=receive,
            device_id=peer, device_id_type=pl.DeviceIdType.MESH,
        ).start()

    def give_head(source, target, which, part, h, own):
        at = part_rows(part)
        for d in range(planes):
            p = lax.rem(plane + d, planes)
            if own and d == 0:
                pltpu.make_async_copy(
                    source.at[h * planes + p, at], target.at[me, at], give_receive.at[which, part]
                ).start()
            else:
                remote(
                    source.at[h * planes + p, at], target.at[me, at],
                    give_send.at[which, part], give_receive.at[which, part],
                    {"seq": p * plane_size + h},
                )

    def give_all(source, target, which, part):
        def one(i, carry):
            give_head(source, target, which, part, lax.rem(spot + turn_of(i), plane_size), False)
            return carry

        lax.fori_loop(0, plane_size - 1, one, 0)
        give_head(source, target, which, part, spot, True)

    def take_all(source, target, which, part):
        at = part_rows(part)
        slot = spot * planes + plane

        def one_spot(z, own):
            for d in range(planes):
                p = lax.rem(plane + d, planes)
                b = p * plane_size + z
                if own and d == 0:
                    pltpu.make_async_copy(
                        source.at[b, at], target.at[slot, at], take_receive.at[which, spot]
                    ).start()
                else:
                    remote(
                        source.at[b, at], target.at[slot, at],
                        take_send.at[which, part], take_receive.at[which, spot], {"seq": b},
                    )

        def one(i, carry):
            one_spot(lax.rem(spot + turn_of(i), plane_size), False)
            return carry

        lax.fori_loop(0, plane_size - 1, one, 0)
        one_spot(spot, True)

    def given(target, which, part):
        some = target.at[:, part_rows(part)]
        pltpu.make_async_copy(some, some, give_receive.at[which, part]).wait()

    def taken(target, which, h):
        some = target.at[slots(h)]
        pltpu.make_async_copy(some, some, take_receive.at[which, h]).wait()

    def sent(target, send):
        some = target.at[pl.ds(0, seq_count - 1), part_rows(0)]
        pltpu.make_async_copy(some, some, send).wait()

    def store_piece(target, h, result):
        target[slots(h)] = result.reshape(planes, rows, DIM)

    def load_state(source, h):
        return source[slots(h)].reshape(DIM, DIM)

    lower = lax.broadcasted_iota(jnp.int32, (BLOCK, BLOCK), 0) >= lax.broadcasted_iota(
        jnp.int32, (BLOCK, BLOCK), 1
    )
    cumulative = lax.dot_general(
        log_ref[...], lower.astype(F32), NT,
        precision=lax.Precision.HIGHEST, preferred_element_type=F32,
    )
    cum_row[...] = cumulative
    turned = jnp.transpose(jnp.concatenate([cumulative] * (DIM // heads), axis=0))
    for h in range(heads):
        spread = jnp.broadcast_to(turned[:, h : h + 1], (BLOCK, DIM))
        cum_col[:, h * DIM : (h + 1) * DIM] = spread
        total = spread[BLOCK - 1 :, :]
        trail[:, h * DIM : (h + 1) * DIM] = jnp.exp(total - spread)
        for p in range(planes):
            own_total[h * planes + p] = total

    loads[0].wait()
    loads[1].wait()

    def make_piece(h, carry):
        at = columns(h)
        high, low = split(key[:, at].astype(F32) * trail[:, at])
        both = value[:, at]
        store_piece(piece, h, mul(high, both, TN) + mul(low, both, TN))
        return carry

    lax.fori_loop(0, heads, make_piece, 0)
    pl.semaphore_wait(barrier, seq_count + head_count - 2)
    give_all(piece, arrived, 0, 0)

    pltpu.make_async_copy(
        own_total.at[spot * planes + plane], totals.at[me], total_sem.at[1]
    ).start()

    def share_total(d, carry):
        peer = lax.rem(me + d, seq_count)
        slot = lax.rem(peer, plane_size) * planes + peer // plane_size
        remote(own_total.at[slot], totals.at[me], total_sem.at[0], total_sem.at[1], {"seq": peer})
        return carry

    lax.fori_loop(1, seq_count, share_total, 0)
    give_all(piece, arrived, 0, 1)

    loads[2].wait()
    loads[3].wait()
    causal = lax.broadcasted_iota(jnp.int32, (HALF, HALF), 0) >= lax.broadcasted_iota(
        jnp.int32, (HALF, HALF), 1
    )

    def forward(h, carry):
        at = columns(h)
        row = cum_row[pl.ds(h, 1), :]
        col = cum_col[:, at]
        top = jnp.concatenate([col[:HALF]] * 2, axis=1)
        low = jnp.concatenate([col[HALF:]] * 2, axis=1)
        left, right = row[:, :HALF], row[:, HALF:]
        masked = -1e30
        d0 = jnp.exp(jnp.where(causal, top - left, masked))
        d1 = jnp.concatenate(
            [jnp.exp(low - left), jnp.exp(jnp.where(causal, low - right, masked))], axis=1
        )
        decay0[h] = d0
        decay1[h] = d1
        keys = key[:, at]
        values = value[:, at]
        w0 = (mul(query[:HALF, at], keys[:HALF], NT) * d0).astype(BF16)
        w1 = (mul(query[HALF:, at], keys, NT) * d1).astype(BF16)
        weight0[h] = w0
        weight1[h] = w1
        out[:HALF, at] = mul(w0, values[:HALF], NN)
        out[HALF:, at] = mul(w1, values, NN)
        return carry

    def advance(part):
        at = part_rows(part)

        def one(b, running):
            before[b, at] = running
            return jnp.exp(totals[b]) * running + arrived[b, at]

        lax.fori_loop(0, seq_count, one, jnp.zeros((half_rows, DIM), F32))

    def prepare(h, carry):
        at = columns(h)
        grown = jnp.exp(cum_col[:, at])
        lead[:, at] = grown
        high, low = split(query[:, at].astype(F32) * grown)
        query_high[:, at] = high
        query_low[:, at] = low
        scaled[:, at] = cot[:, at].astype(F32) * gain_ref[:, at]
        return carry

    lax.fori_loop(0, early, forward, 0)
    pltpu.make_async_copy(totals, totals, total_sem.at[1]).wait()
    given(arrived, 0, 0)
    advance(0)
    take_all(before, state, 0, 0)
    lax.fori_loop(early, heads, forward, 0)
    given(arrived, 0, 1)
    advance(1)
    take_all(before, state, 0, 1)
    lax.fori_loop(0, heads, prepare, 0)

    def finish_out(i, carry):
        squares, inners = carry
        h = lax.rem(spot + plane_size - turn_of(i), plane_size)
        taken(state, 0, h)
        at = columns(h)
        high, low = split(load_state(state, h))
        outer = mul(query[:, at], jnp.concatenate([high, low], axis=1), NN)
        whole = out[:, at] + lead[:, at] * (outer[:, :DIM] + outer[:, DIM:])
        out[:, at] = whole
        return squares + whole * whole, inners + scaled[:, at] * whole

    zero = jnp.zeros((BLOCK, DIM), F32)
    squares, inners = lax.fori_loop(0, heads, finish_out, (zero, zero))
    square_row = jnp.sum(jnp.transpose(squares), axis=0, keepdims=True)
    inner_row = jnp.sum(jnp.transpose(inners), axis=0, keepdims=True)
    for i in range(BLOCK // DIM):
        stat[i : i + 1, :] = square_row[:, i * DIM : (i + 1) * DIM]
        stat[4 + i : 5 + i, :] = inner_row[:, i * DIM : (i + 1) * DIM]
    pltpu.make_async_copy(stat, stats.at[place], stat_sem.at[1]).start()

    def share_stat(d, carry):
        peer = lax.rem(place + d, head_count)
        remote(stat, stats.at[place], stat_sem.at[0], stat_sem.at[1], {"head": peer})
        return carry

    lax.fori_loop(1, head_count, share_stat, 0)
    pltpu.make_async_copy(stats, stats, stat_sem.at[1]).wait()
    summed = stats[0]
    for i in range(1, head_count):
        summed = summed + stats[i]
    inverse_rows = lax.rsqrt(summed[:4] / features + EPSILON)
    mean_rows = inverse_rows * summed[4:] / features

    def to_columns(four):
        return jnp.concatenate(
            [jnp.transpose(jnp.broadcast_to(four[i : i + 1], (DIM, DIM))) for i in range(4)], axis=0
        )

    inverse = to_columns(inverse_rows)
    mean_term = to_columns(mean_rows)

    def make_grad(i, carry):
        h = lax.rem(spot + turn_of(i), plane_size)
        at = columns(h)
        normed = out[:, at] * inverse
        out[:, at] = normed
        g = (inverse * (scaled[:, at] - normed * mean_term)).astype(BF16)
        grad[:, at] = g
        store_piece(
            grad_piece, h, mul(query_high[:, at], g, TN) + mul(query_low[:, at], g, TN)
        )
        return h

    def make_and_give(i, carry):
        give_head(grad_piece, grad_arrived, 1, 0, make_grad(i, carry), False)
        return carry

    lax.fori_loop(0, heads - 1, make_and_give, 0)
    make_grad(heads - 1, 0)
    give_head(grad_piece, grad_arrived, 1, 0, spot, True)
    give_all(grad_piece, grad_arrived, 1, 1)

    def backward(h, carry):
        at = columns(h)
        d0 = decay0[h]
        d1 = decay1[h]
        keys = key[:, at]
        values = value[:, at]
        g = grad[:, at]
        q = query[:, at]
        w0 = weight0[h]
        w1 = weight1[h]
        att[:, at] = (out[:, at] * gain_ref[:, at]).astype(BF16)
        g0 = (mul(g[:HALF], values[:HALF], NT) * d0).astype(BF16)
        g1 = (mul(g[HALF:], values, NT) * d1).astype(BF16)
        high, low = split(load_state(state, h))
        outer = lead[:, at] * (mul(g, high, NT) + mul(g, low, NT))
        gq[:HALF, at] = (mul(g0, keys[:HALF], NN) + outer[:HALF]).astype(BF16)
        gq[HALF:, at] = (mul(g1, keys, NN) + outer[HALF:]).astype(BF16)
        full_key = mul(g1, q[HALF:], TN)
        full_value = mul(w1, g[HALF:], TN)
        inner_key[:HALF, at] = full_key[:HALF] + mul(g0, q[:HALF], TN)
        inner_key[HALF:, at] = full_key[HALF:]
        inner_value[:HALF, at] = full_value[:HALF] + mul(w0, g[:HALF], TN)
        inner_value[HALF:, at] = full_value[HALF:]
        return carry

    def retreat(part):
        at = part_rows(part)

        def one(turn, running):
            b = seq_count - 1 - turn
            after[b, at] = running
            return grad_arrived[b, at] + jnp.exp(totals[b]) * running

        lax.fori_loop(0, seq_count, one, jnp.zeros((half_rows, DIM), F32))

    lax.fori_loop(0, early_back, backward, 0)
    given(grad_arrived, 1, 0)
    retreat(0)
    take_all(after, after_state, 1, 0)
    lax.fori_loop(early_back, early_back + 2, backward, 0)
    given(grad_arrived, 1, 1)
    retreat(1)
    take_all(after, after_state, 1, 1)
    lax.fori_loop(early_back + 2, heads, backward, 0)

    def finish(i, carry):
        h = lax.rem(spot + plane_size - turn_of(i), plane_size)
        taken(after_state, 1, h)
        at = columns(h)
        high, low = split(load_state(after_state, h))
        shrunk = trail[:, at]
        values = value[:, at]
        from_value = mul(values, high, NT) + mul(values, low, NT)
        gk[:, at] = (inner_key[:, at] + shrunk * from_value).astype(BF16)
        from_key = mul(key[:, at], jnp.concatenate([high, low], axis=1), NN)
        gv[:, at] = (
            inner_value[:, at] + shrunk * (from_key[:, :DIM] + from_key[:, DIM:])
        ).astype(BF16)
        return carry

    lax.fori_loop(0, heads, finish, 0)

    some = totals.at[pl.ds(0, seq_count - 1)]
    pltpu.make_async_copy(some, some, total_sem.at[0]).wait()
    some = stats.at[pl.ds(0, head_count - 1)]
    pltpu.make_async_copy(some, some, stat_sem.at[0]).wait()
    for which in range(2):
        for part in range(2):
            sent(piece, give_send.at[which, part])
            sent(piece, take_send.at[which, part])


def on_device(seq_count, head_count, queries, key_vecs, value_vecs, log_decay, norm_gain, cotangent):
    tokens, width = queries.shape
    heads = width // DIM
    rows = heads * DIM // seq_count
    planes = seq_count // heads
    vmem = pl.BlockSpec(memory_space=pltpu.VMEM)
    hbm = pl.BlockSpec(memory_space=pltpu.HBM)
    narrow = pltpu.VMEM((tokens, width), BF16)
    wide = pltpu.VMEM((tokens, width), F32)
    chunk = pltpu.VMEM((seq_count, rows, DIM), F32)
    line = pltpu.VMEM((seq_count, 1, DIM), F32)
    pair = pltpu.SemaphoreType.DMA((2,))
    square = pltpu.SemaphoreType.DMA((2, 2))
    results = pl.pallas_call(
        functools.partial(kernel, planes, heads, head_count, heads, 4, 3),
        out_shape=(narrow,) * 4,
        in_specs=[vmem, vmem] + [hbm] * 4,
        out_specs=(vmem,) * 4,
        scratch_shapes=[narrow] * 4
        + [
            pltpu.VMEM((heads, tokens), F32),
            wide,
            wide,
            wide,
            pltpu.VMEM((heads, HALF, HALF), F32),
            pltpu.VMEM((heads, HALF, BLOCK), F32),
            pltpu.VMEM((heads, HALF, HALF), BF16),
            pltpu.VMEM((heads, HALF, BLOCK), BF16),
            wide,
            wide,
            narrow,
            narrow,
            narrow,
            wide,
            wide,
            line,
            line,
        ]
        + [chunk] * 8
        + [pltpu.VMEM((8, DIM), F32), pltpu.VMEM((head_count, 8, DIM), F32)]
        + [pltpu.SemaphoreType.DMA((4,)), pair, pair, square, square, square]
        + [pltpu.SemaphoreType.DMA((2, heads))],
        compiler_params=pltpu.CompilerParams(
            collective_id=0, has_side_effects=True, vmem_limit_bytes=59 * 1024 * 1024
        ),
    )(log_decay.T, norm_gain.reshape(1, width), queries, key_vecs, value_vecs, cotangent)
    return pl.pallas_call(
        store_kernel,
        out_shape=(jax.ShapeDtypeStruct((tokens, width), BF16),) * 4,
        in_specs=[vmem] * 4,
        out_specs=(hbm,) * 4,
        scratch_shapes=[pltpu.SemaphoreType.DMA((4,))],
        compiler_params=pltpu.CompilerParams(vmem_limit_bytes=8 * 1024 * 1024),
    )(*results)


def solution(mesh):
    return jax.shard_map(
        functools.partial(on_device, mesh.shape["seq"], mesh.shape["head"]),
        mesh=mesh,
        in_specs=(
            P("seq", "head"),
            P("seq", "head"),
            P("seq", "head"),
            P("seq", "head"),
            P("head"),
            P("seq", "head"),
        ),
        out_specs=(P("seq", "head"), P("seq", "head"), P("seq", "head"), P("seq", "head")),
        check_vma=False,
    )
```

```python
import functools

import jax
import jax.numpy as jnp
from jax import lax
from jax.experimental import pallas as pl
from jax.experimental.pallas import tpu as pltpu
from jax.sharding import PartitionSpec as P

DIM = 128
BLOCK = 512
HALF = 256
PARTS = 2
EPSILON = 1e-06
F32 = jnp.float32
BF16 = jnp.bfloat16
NN = (((1,), (0,)), ((), ()))
NT = (((1,), (1,)), ((), ()))
TN = (((0,), (0,)), ((), ()))


def mul(a, b, dims):
    return lax.dot_general(a, b, dims, preferred_element_type=F32)


def split(x):
    high = x.astype(BF16)
    return high, (x - high.astype(F32)).astype(BF16)


def store_kernel(*refs):
    sources, targets, sem = refs[:4], refs[4:8], refs[8]
    copies = [
        pltpu.make_async_copy(source, target, sem.at[i])
        for i, (source, target) in enumerate(zip(sources, targets))
    ]
    for copy in copies:
        copy.start()
    for copy in copies:
        copy.wait()


def kernel(
    parts, planes, plane_size, head_count, heads,
    log_hbm, gain_hbm, query_hbm, key_hbm, value_hbm, cot_hbm,
    att, gq, gk, gv,
    log_ref, gain_ref, query, key, value, cot,
    cum_row, cum_col, lead, trail, decay0, decay1, weight0, weight1,
    out, scaled, turned_query, grad, inner_key, inner_value,
    own_total, totals,
    piece, arrived, before, state,
    grad_piece, grad_arrived, after, after_state,
    stat, stats,
    in_sem, total_sem, stat_sem, give_send, give_receive, take_send, take_receive,
):
    me = lax.axis_index("seq")
    plane = me // plane_size
    spot = lax.rem(me, plane_size)
    place = lax.axis_index("head")
    seq_count = planes * plane_size
    rows = piece.shape[1]
    part_size = rows // parts
    features = head_count * heads * DIM

    barrier = pltpu.get_barrier_semaphore()

    def greet_seq(d, carry):
        pl.semaphore_signal(
            barrier, inc=1, device_id={"seq": lax.rem(me + d + seq_count // 2, seq_count)},
            device_id_type=pl.DeviceIdType.MESH,
        )
        return carry

    def greet_head(d, carry):
        pl.semaphore_signal(
            barrier, inc=1, device_id={"head": lax.rem(place + d, head_count)},
            device_id_type=pl.DeviceIdType.MESH,
        )
        return carry

    lax.fori_loop(0, seq_count // 2, greet_seq, 0)
    lax.fori_loop(seq_count // 2 + 1, seq_count, greet_seq, 0)
    lax.fori_loop(1, head_count, greet_head, 0)
    loads = [
        pltpu.make_async_copy(source, target, in_sem.at[i])
        for i, (source, target) in enumerate(
            (
                (log_hbm, log_ref), (key_hbm, key), (value_hbm, value),
                (query_hbm, query), (cot_hbm, cot), (gain_hbm, gain_ref),
            )
        )
    ]
    for load in loads:
        load.start()

    def columns(h):
        return pl.ds(pl.multiple_of(h * DIM, DIM), DIM)

    def turn_of(i):
        return plane_size // 2 + (1 - 2 * lax.rem(i, 2)) * ((i + 1) // 2)

    def part_rows(part):
        return pl.ds(part * part_size, part_size)

    def slots(h):
        return pl.ds(pl.multiple_of(h * planes, planes), planes)

    def remote(source, target, send, receive, peer):
        pltpu.make_async_remote_copy(
            src_ref=source, dst_ref=target, send_sem=send, recv_sem=receive,
            device_id=peer, device_id_type=pl.DeviceIdType.MESH,
        ).start()

    def give_head(source, target, which, part, h, own):
        at = part_rows(part)
        for d in range(planes):
            p = lax.rem(plane + d, planes)
            if own and d == 0:
                pltpu.make_async_copy(
                    source.at[h * planes + p, at], target.at[me, at], give_receive.at[which, part]
                ).start()
            else:
                remote(
                    source.at[h * planes + p, at], target.at[me, at],
                    give_send.at[which, part], give_receive.at[which, part],
                    {"seq": p * plane_size + h},
                )

    def give_all(source, target, which, part):
        def one(i, carry):
            give_head(source, target, which, part, lax.rem(spot + turn_of(i), plane_size), False)
            return carry

        lax.fori_loop(0, plane_size - 1, one, 0)
        give_head(source, target, which, part, spot, True)

    def take_all(source, target, which, part):
        at = part_rows(part)
        slot = spot * planes + plane

        def one_spot(z, own):
            for d in range(planes):
                p = lax.rem(plane + d, planes)
                b = p * plane_size + z
                if own and d == 0:
                    pltpu.make_async_copy(
                        source.at[b, at], target.at[slot, at], take_receive.at[which, spot]
                    ).start()
                else:
                    remote(
                        source.at[b, at], target.at[slot, at],
                        take_send.at[which, part], take_receive.at[which, spot], {"seq": b},
                    )

        def one(i, carry):
            one_spot(lax.rem(spot + turn_of(i), plane_size), False)
            return carry

        lax.fori_loop(0, plane_size - 1, one, 0)
        one_spot(spot, True)

    def given(target, which, part):
        some = target.at[:, part_rows(part)]
        pltpu.make_async_copy(some, some, give_receive.at[which, part]).wait()

    def taken(target, which, h):
        some = target.at[slots(h)]
        pltpu.make_async_copy(some, some, take_receive.at[which, h]).wait()

    def sent(target, send):
        some = target.at[pl.ds(0, seq_count - 1), part_rows(0)]
        pltpu.make_async_copy(some, some, send).wait()

    def store_piece(target, h, result):
        target[slots(h)] = result.reshape(planes, rows, DIM)

    def load_state(source, h):
        return source[slots(h)].reshape(DIM, DIM)

    lower = lax.broadcasted_iota(jnp.int32, (BLOCK, BLOCK), 0) >= lax.broadcasted_iota(
        jnp.int32, (BLOCK, BLOCK), 1
    )
    lower = lower.astype(F32).astype(BF16)
    loads[0].wait()
    logs = log_ref[...]
    high, low = split(logs)
    rest = (logs - high.astype(F32) - low.astype(F32)).astype(BF16)
    terms = mul(jnp.concatenate([high, low, rest], axis=0), lower, NT)
    cumulative = terms[:heads] + (terms[heads : 2 * heads] + terms[2 * heads :])
    cum_row[...] = cumulative
    turned = jnp.transpose(jnp.concatenate([cumulative] * (DIM // heads), axis=0))
    for h in range(heads):
        spread = jnp.broadcast_to(turned[:, h : h + 1], (BLOCK, DIM))
        cum_col[:, h * DIM : (h + 1) * DIM] = spread
        total = spread[BLOCK - 1 :, :]
        trail[:, h * DIM : (h + 1) * DIM] = jnp.exp(total - spread)
        for p in range(planes):
            own_total[h * planes + p] = total

    loads[1].wait()
    loads[2].wait()

    def make_piece(h, carry):
        at = columns(h)
        high, low = split(key[:, at].astype(F32) * trail[:, at])
        both = value[:, at]
        store_piece(piece, h, mul(high, both, TN) + mul(low, both, TN))
        return carry

    def head_at(i):
        return lax.rem(spot + turn_of(i), plane_size)

    def make_and_give_piece(i, carry):
        give_head(piece, arrived, 0, 0, head_at(i), False)
        make_piece(head_at(i + 1), carry)
        return carry

    make_piece(head_at(0), 0)
    pl.semaphore_wait(barrier, seq_count + head_count - 2)
    lax.fori_loop(0, heads - 1, make_and_give_piece, 0)
    give_head(piece, arrived, 0, 0, spot, True)

    pltpu.make_async_copy(
        own_total.at[spot * planes + plane], totals.at[me], total_sem.at[1]
    ).start()

    def share_total(d, carry):
        peer = lax.rem(me + d, seq_count)
        slot = lax.rem(peer, plane_size) * planes + peer // plane_size
        remote(own_total.at[slot], totals.at[me], total_sem.at[0], total_sem.at[1], {"seq": peer})
        return carry

    lax.fori_loop(1, seq_count, share_total, 0)
    for part in range(1, parts):
        give_all(piece, arrived, 0, part)

    for load in loads[3:]:
        load.wait()
    causal = lax.broadcasted_iota(jnp.int32, (HALF, HALF), 0) >= lax.broadcasted_iota(
        jnp.int32, (HALF, HALF), 1
    )

    def forward(h, carry):
        at = columns(h)
        row = cum_row[pl.ds(h, 1), :]
        col = cum_col[:, at]
        top = jnp.concatenate([col[:HALF]] * 2, axis=1)
        low = jnp.concatenate([col[HALF:]] * 2, axis=1)
        left, right = row[:, :HALF], row[:, HALF:]
        masked = -1e30
        d0 = jnp.exp(jnp.where(causal, top - left, masked))
        d1 = jnp.concatenate(
            [jnp.exp(low - left), jnp.exp(jnp.where(causal, low - right, masked))], axis=1
        )
        decay0[h] = d0
        decay1[h] = d1
        keys = key[:, at]
        values = value[:, at]
        w0 = (mul(query[:HALF, at], keys[:HALF], NT) * d0).astype(BF16)
        w1 = (mul(query[HALF:, at], keys, NT) * d1).astype(BF16)
        weight0[h] = w0
        weight1[h] = w1
        out[:HALF, at] = mul(w0, values[:HALF], NN)
        out[HALF:, at] = mul(w1, values, NN)
        return carry

    def advance(part):
        at = part_rows(part)

        def one(b, running):
            before[b, at] = running
            return totals[b] * running + arrived[b, at]

        lax.fori_loop(0, seq_count, one, jnp.zeros((part_size, DIM), F32), unroll=4)

    def prepare(h, carry):
        at = columns(h)
        grown = jnp.exp(cum_col[:, at])
        lead[:, at] = grown
        high, low = split(jnp.transpose(query[:, at].astype(F32) * grown))
        turned_query[h] = jnp.concatenate([high, low], axis=0)
        scaled[:, at] = cot[:, at].astype(F32) * gain_ref[:, at]
        return carry

    lax.fori_loop(0, heads, forward, 0)
    lax.fori_loop(0, heads, prepare, 0)
    pltpu.make_async_copy(totals, totals, total_sem.at[1]).wait()
    totals[...] = jnp.exp(totals[...])
    for part in range(parts):
        given(arrived, 0, part)
        advance(part)
        take_all(before, state, 0, part)

    def finish_out(i, carry):
        squares, inners = carry
        h = lax.rem(spot + plane_size - turn_of(i), plane_size)
        taken(state, 0, h)
        at = columns(h)
        high, low = split(load_state(state, h))
        outer = mul(query[:, at], jnp.concatenate([high, low], axis=1), NN)
        whole = out[:, at] + lead[:, at] * (outer[:, :DIM] + outer[:, DIM:])
        out[:, at] = whole
        return squares + whole * whole, inners + scaled[:, at] * whole

    zero = jnp.zeros((BLOCK, DIM), F32)
    squares, inners = lax.fori_loop(0, heads, finish_out, (zero, zero))
    lanes = lax.broadcasted_iota(jnp.int32, (DIM, DIM), 1)
    packed = jnp.zeros((DIM, DIM), F32)
    for which, sums in enumerate((squares, inners)):
        sums = jnp.sum(sums, axis=1, keepdims=True)
        for i in range(BLOCK // DIM):
            packed = jnp.where(lanes == 4 * which + i, sums[i * DIM : (i + 1) * DIM], packed)
    stat[...] = jnp.transpose(packed)[:8]
    pltpu.make_async_copy(stat, stats.at[place], stat_sem.at[1]).start()

    def share_stat(d, carry):
        peer = lax.rem(place + d, head_count)
        remote(stat, stats.at[place], stat_sem.at[0], stat_sem.at[1], {"head": peer})
        return carry

    lax.fori_loop(1, head_count, share_stat, 0)
    pltpu.make_async_copy(stats, stats, stat_sem.at[1]).wait()
    summed = stats[0]
    for i in range(1, head_count):
        summed = summed + stats[i]
    inverse_rows = lax.rsqrt(summed[:4] / features + EPSILON)
    mean_rows = inverse_rows * summed[4:] / features

    turned = jnp.transpose(jnp.concatenate([inverse_rows, mean_rows] * (DIM // 8), axis=0))

    def to_columns(first):
        return jnp.concatenate(
            [jnp.broadcast_to(turned[:, i : i + 1], (DIM, DIM)) for i in range(first, first + 4)], axis=0
        )

    inverse = to_columns(0)
    mean_term = to_columns(4)

    def make_grad(i, carry):
        h = lax.rem(spot + turn_of(i), plane_size)
        at = columns(h)
        normed = out[:, at] * inverse
        out[:, at] = normed
        g = (inverse * (scaled[:, at] - normed * mean_term)).astype(BF16)
        grad[:, at] = g
        both = mul(turned_query[h], g, NN)
        store_piece(grad_piece, h, both[:DIM] + both[DIM:])
        return h

    def make_and_give(i, carry):
        give_head(grad_piece, grad_arrived, 1, 0, make_grad(i, carry), False)
        return carry

    lax.fori_loop(0, heads - 1, make_and_give, 0)
    make_grad(heads - 1, 0)
    give_head(grad_piece, grad_arrived, 1, 0, spot, True)
    for part in range(1, parts):
        give_all(grad_piece, grad_arrived, 1, part)

    def backward(h, carry):
        at = columns(h)
        d0 = decay0[h]
        d1 = decay1[h]
        keys = key[:, at]
        values = value[:, at]
        g = grad[:, at]
        q = query[:, at]
        w0 = weight0[h]
        w1 = weight1[h]
        att[:, at] = (out[:, at] * gain_ref[:, at]).astype(BF16)
        g0 = (mul(g[:HALF], values[:HALF], NT) * d0).astype(BF16)
        g1 = (mul(g[HALF:], values, NT) * d1).astype(BF16)
        high, low = split(load_state(state, h))
        outer = lead[:, at] * (mul(g, high, NT) + mul(g, low, NT))
        gq[:HALF, at] = (mul(g0, keys[:HALF], NN) + outer[:HALF]).astype(BF16)
        gq[HALF:, at] = (mul(g1, keys, NN) + outer[HALF:]).astype(BF16)
        full_key = mul(g1, q[HALF:], TN)
        full_value = mul(w1, g[HALF:], TN)
        inner_key[:HALF, at] = full_key[:HALF] + mul(g0, q[:HALF], TN)
        inner_key[HALF:, at] = full_key[HALF:]
        inner_value[:HALF, at] = full_value[:HALF] + mul(w0, g[:HALF], TN)
        inner_value[HALF:, at] = full_value[HALF:]
        return carry

    def retreat(part):
        at = part_rows(part)

        def one(turn, running):
            b = seq_count - 1 - turn
            after[b, at] = running
            return grad_arrived[b, at] + totals[b] * running

        lax.fori_loop(0, seq_count, one, jnp.zeros((part_size, DIM), F32), unroll=4)

    lax.fori_loop(0, heads, backward, 0)
    for part in range(parts):
        given(grad_arrived, 1, part)
        retreat(part)
        take_all(after, after_state, 1, part)

    def finish(i, carry):
        h = lax.rem(spot + plane_size - turn_of(i), plane_size)
        taken(after_state, 1, h)
        at = columns(h)
        high, low = split(load_state(after_state, h))
        shrunk = trail[:, at]
        values = value[:, at]
        from_value = mul(values, high, NT) + mul(values, low, NT)
        gk[:, at] = (inner_key[:, at] + shrunk * from_value).astype(BF16)
        from_key = mul(key[:, at], jnp.concatenate([high, low], axis=1), NN)
        gv[:, at] = (
            inner_value[:, at] + shrunk * (from_key[:, :DIM] + from_key[:, DIM:])
        ).astype(BF16)
        return carry

    lax.fori_loop(0, heads, finish, 0)

    some = totals.at[pl.ds(0, seq_count - 1)]
    pltpu.make_async_copy(some, some, total_sem.at[0]).wait()
    some = stats.at[pl.ds(0, head_count - 1)]
    pltpu.make_async_copy(some, some, stat_sem.at[0]).wait()
    for which in range(2):
        for part in range(parts):
            sent(piece, give_send.at[which, part])
            sent(piece, take_send.at[which, part])


def on_device(seq_count, head_count, queries, key_vecs, value_vecs, log_decay, norm_gain, cotangent):
    tokens, width = queries.shape
    heads = width // DIM
    rows = heads * DIM // seq_count
    planes = seq_count // heads
    vmem = pl.BlockSpec(memory_space=pltpu.VMEM)
    hbm = pl.BlockSpec(memory_space=pltpu.HBM)
    narrow = pltpu.VMEM((tokens, width), BF16)
    wide = pltpu.VMEM((tokens, width), F32)
    chunk = pltpu.VMEM((seq_count, rows, DIM), F32)
    line = pltpu.VMEM((seq_count, 1, DIM), F32)
    pair = pltpu.SemaphoreType.DMA((2,))
    square = pltpu.SemaphoreType.DMA((2, PARTS))
    results = pl.pallas_call(
        functools.partial(kernel, PARTS, planes, heads, head_count, heads),
        out_shape=(narrow,) * 4,
        in_specs=[hbm] * 6,
        out_specs=(vmem,) * 4,
        scratch_shapes=[pltpu.VMEM((heads, tokens), F32), pltpu.VMEM((1, width), F32)]
        + [narrow] * 4
        + [
            pltpu.VMEM((heads, tokens), F32),
            wide,
            wide,
            wide,
            pltpu.VMEM((heads, HALF, HALF), F32),
            pltpu.VMEM((heads, HALF, BLOCK), F32),
            pltpu.VMEM((heads, HALF, HALF), BF16),
            pltpu.VMEM((heads, HALF, BLOCK), BF16),
            wide,
            wide,
            pltpu.VMEM((heads, 2 * DIM, tokens), BF16),
            narrow,
            wide,
            wide,
            line,
            line,
        ]
        + [chunk] * 8
        + [pltpu.VMEM((8, DIM), F32), pltpu.VMEM((head_count, 8, DIM), F32)]
        + [pltpu.SemaphoreType.DMA((6,)), pair, pair, square, square, square]
        + [pltpu.SemaphoreType.DMA((2, heads))],
        compiler_params=pltpu.CompilerParams(
            collective_id=0, has_side_effects=True, vmem_limit_bytes=59 * 1024 * 1024
        ),
    )(log_decay.T, norm_gain.reshape(1, width), queries, key_vecs, value_vecs, cotangent)
    return pl.pallas_call(
        store_kernel,
        out_shape=(jax.ShapeDtypeStruct((tokens, width), BF16),) * 4,
        in_specs=[vmem] * 4,
        out_specs=(hbm,) * 4,
        scratch_shapes=[pltpu.SemaphoreType.DMA((4,))],
        compiler_params=pltpu.CompilerParams(vmem_limit_bytes=8 * 1024 * 1024),
    )(*results)


def solution(mesh):
    return jax.shard_map(
        functools.partial(on_device, mesh.shape["seq"], mesh.shape["head"]),
        mesh=mesh,
        in_specs=(
            P("seq", "head"),
            P("seq", "head"),
            P("seq", "head"),
            P("seq", "head"),
            P("head"),
            P("seq", "head"),
        ),
        out_specs=(P("seq", "head"), P("seq", "head"), P("seq", "head"), P("seq", "head")),
        check_vma=False,
    )
```

```python
import functools

import jax
import jax.numpy as jnp
from jax import lax
from jax.experimental import pallas as pl
from jax.experimental.pallas import tpu as pltpu
from jax.sharding import PartitionSpec as P

DIM = 128
BLOCK = 512
HALF = 256
PARTS = 2
EPSILON = 1e-06
F32 = jnp.float32
BF16 = jnp.bfloat16
NN = (((1,), (0,)), ((), ()))
NT = (((1,), (1,)), ((), ()))
TN = (((0,), (0,)), ((), ()))


def mul(a, b, dims):
    return lax.dot_general(a, b, dims, preferred_element_type=F32)


def split(x):
    high = x.astype(BF16)
    return high, (x - high.astype(F32)).astype(BF16)


def store_kernel(*refs):
    sources, targets, sem = refs[:4], refs[4:8], refs[8]
    copies = [
        pltpu.make_async_copy(source, target, sem.at[i])
        for i, (source, target) in enumerate(zip(sources, targets))
    ]
    for copy in copies:
        copy.start()
    for copy in copies:
        copy.wait()


def kernel(
    parts, planes, plane_size, head_count, heads,
    log_hbm, gain_hbm, query_hbm, key_hbm, value_hbm, cot_hbm,
    att, gq, gk, gv,
    log_ref, gain_ref, query, key, value, cot,
    cum_row, cum_col, lead, trail, decay0, decay1, weight0, weight1,
    out, scaled, turned_query, grad, inner_key, inner_value,
    own_total, totals,
    piece, arrived, before, state,
    grad_piece, grad_arrived, after, after_state,
    stat, stats,
    in_sem, total_sem, stat_sem, give_send, give_receive, take_send, take_receive,
):
    me = lax.axis_index("seq")
    plane = me // plane_size
    spot = lax.rem(me, plane_size)
    place = lax.axis_index("head")
    seq_count = planes * plane_size
    rows = piece.shape[1]
    part_size = rows // parts
    features = head_count * heads * DIM

    barrier = pltpu.get_barrier_semaphore()

    def greet_seq(d, carry):
        pl.semaphore_signal(
            barrier, inc=1, device_id={"seq": lax.rem(me + d + seq_count // 2, seq_count)},
            device_id_type=pl.DeviceIdType.MESH,
        )
        return carry

    def greet_head(d, carry):
        pl.semaphore_signal(
            barrier, inc=1, device_id={"head": lax.rem(place + d, head_count)},
            device_id_type=pl.DeviceIdType.MESH,
        )
        return carry

    lax.fori_loop(0, seq_count // 2, greet_seq, 0)
    lax.fori_loop(seq_count // 2 + 1, seq_count, greet_seq, 0)
    lax.fori_loop(1, head_count, greet_head, 0)
    loads = [
        pltpu.make_async_copy(source, target, in_sem.at[i])
        for i, (source, target) in enumerate(
            (
                (log_hbm, log_ref), (key_hbm, key), (value_hbm, value),
                (query_hbm, query), (cot_hbm, cot), (gain_hbm, gain_ref),
            )
        )
    ]
    for load in loads:
        load.start()

    def columns(h):
        return pl.ds(pl.multiple_of(h * DIM, DIM), DIM)

    def turn_of(i):
        return lax.rem(plane_size // 2 + (1 - 2 * lax.rem(place, 2)) * (1 - 2 * lax.rem(i, 2)) * ((i + 1) // 2), plane_size)

    def part_rows(part):
        return pl.ds(part * part_size, part_size)

    def slots(h):
        return pl.ds(pl.multiple_of(h * planes, planes), planes)

    def remote(source, target, send, receive, peer):
        pltpu.make_async_remote_copy(
            src_ref=source, dst_ref=target, send_sem=send, recv_sem=receive,
            device_id=peer, device_id_type=pl.DeviceIdType.MESH,
        ).start()

    def give_head(source, target, which, part, h, own):
        at = part_rows(part)
        for d in (2, 1, 3, 0):
            p = lax.rem(plane + d * (1 + 2 * lax.rem(place, 2)), planes)
            if own and d == 0:
                pltpu.make_async_copy(
                    source.at[h * planes + p, at], target.at[me, at], give_receive.at[which, part]
                ).start()
            else:
                remote(
                    source.at[h * planes + p, at], target.at[me, at],
                    give_send.at[which, part], give_receive.at[which, part],
                    {"seq": p * plane_size + h},
                )

    def give_all(source, target, which, part):
        def one(i, carry):
            give_head(source, target, which, part, lax.rem(spot + turn_of(i), plane_size), False)
            return carry

        lax.fori_loop(0, plane_size - 1, one, 0)
        give_head(source, target, which, part, spot, True)

    def take_all(source, target, which, part):
        at = part_rows(part)
        slot = spot * planes + plane

        def one_spot(z, own):
            for d in (2, 1, 3, 0):
                p = lax.rem(plane + d * (1 + 2 * lax.rem(place, 2)), planes)
                b = p * plane_size + z
                if own and d == 0:
                    pltpu.make_async_copy(
                        source.at[b, at], target.at[slot, at], take_receive.at[which, spot]
                    ).start()
                else:
                    remote(
                        source.at[b, at], target.at[slot, at],
                        take_send.at[which, part], take_receive.at[which, spot], {"seq": b},
                    )

        def one(i, carry):
            one_spot(lax.rem(spot + turn_of(i), plane_size), False)
            return carry

        lax.fori_loop(0, plane_size - 1, one, 0)
        one_spot(spot, True)

    def given(target, which, part):
        some = target.at[:, part_rows(part)]
        pltpu.make_async_copy(some, some, give_receive.at[which, part]).wait()

    def taken(target, which, h):
        some = target.at[slots(h)]
        pltpu.make_async_copy(some, some, take_receive.at[which, h]).wait()

    def sent(target, send):
        some = target.at[pl.ds(0, seq_count - 1), part_rows(0)]
        pltpu.make_async_copy(some, some, send).wait()

    def store_piece(target, h, result):
        target[slots(h)] = result.reshape(planes, rows, DIM)

    def load_state(source, h):
        return source[slots(h)].reshape(DIM, DIM)

    lower = lax.broadcasted_iota(jnp.int32, (BLOCK, BLOCK), 0) >= lax.broadcasted_iota(
        jnp.int32, (BLOCK, BLOCK), 1
    )
    lower = lower.astype(F32).astype(BF16)
    loads[0].wait()
    logs = log_ref[...]
    high, low = split(logs)
    rest = (logs - high.astype(F32) - low.astype(F32)).astype(BF16)
    terms = mul(jnp.concatenate([high, low, rest], axis=0), lower, NT)
    cumulative = terms[:heads] + (terms[heads : 2 * heads] + terms[2 * heads :])
    cum_row[...] = cumulative
    turned = jnp.transpose(jnp.concatenate([cumulative] * (DIM // heads), axis=0))
    for h in range(heads):
        spread = jnp.broadcast_to(turned[:, h : h + 1], (BLOCK, DIM))
        cum_col[:, h * DIM : (h + 1) * DIM] = spread
        total = spread[BLOCK - 1 :, :]
        trail[:, h * DIM : (h + 1) * DIM] = jnp.exp(total - spread)
        for p in range(planes):
            own_total[h * planes + p] = total

    loads[1].wait()
    loads[2].wait()

    def make_piece(h, carry):
        at = columns(h)
        high, low = split(key[:, at].astype(F32) * trail[:, at])
        both = value[:, at]
        store_piece(piece, h, mul(high, both, TN) + mul(low, both, TN))
        return carry

    def head_at(i):
        return lax.rem(spot + turn_of(i), plane_size)

    def make_and_give_piece(i, carry):
        give_head(piece, arrived, 0, 0, head_at(i), False)
        make_piece(head_at(i + 1), carry)
        return carry

    make_piece(head_at(0), 0)
    pl.semaphore_wait(barrier, seq_count + head_count - 2)
    lax.fori_loop(0, heads - 1, make_and_give_piece, 0)
    give_head(piece, arrived, 0, 0, spot, True)

    pltpu.make_async_copy(
        own_total.at[spot * planes + plane], totals.at[me], total_sem.at[1]
    ).start()

    def share_total(d, carry):
        peer = lax.rem(me + d, seq_count)
        slot = lax.rem(peer, plane_size) * planes + peer // plane_size
        remote(own_total.at[slot], totals.at[me], total_sem.at[0], total_sem.at[1], {"seq": peer})
        return carry

    lax.fori_loop(1, seq_count, share_total, 0)
    for part in range(1, parts):
        give_all(piece, arrived, 0, part)

    for load in loads[3:]:
        load.wait()
    causal = lax.broadcasted_iota(jnp.int32, (HALF, HALF), 0) >= lax.broadcasted_iota(
        jnp.int32, (HALF, HALF), 1
    )

    def forward(h, carry):
        at = columns(h)
        row = cum_row[pl.ds(h, 1), :]
        col = cum_col[:, at]
        top = jnp.concatenate([col[:HALF]] * 2, axis=1)
        low = jnp.concatenate([col[HALF:]] * 2, axis=1)
        left, right = row[:, :HALF], row[:, HALF:]
        masked = -1e30
        d0 = jnp.exp(jnp.where(causal, top - left, masked))
        d1 = jnp.concatenate(
            [jnp.exp(low - left), jnp.exp(jnp.where(causal, low - right, masked))], axis=1
        )
        decay0[h] = d0
        decay1[h] = d1
        keys = key[:, at]
        values = value[:, at]
        w0 = (mul(query[:HALF, at], keys[:HALF], NT) * d0).astype(BF16)
        w1 = (mul(query[HALF:, at], keys, NT) * d1).astype(BF16)
        weight0[h] = w0
        weight1[h] = w1
        out[:HALF, at] = mul(w0, values[:HALF], NN)
        out[HALF:, at] = mul(w1, values, NN)
        return carry

    def advance(part):
        at = part_rows(part)

        def one(b, running):
            before[b, at] = running
            return totals[b] * running + arrived[b, at]

        lax.fori_loop(0, seq_count, one, jnp.zeros((part_size, DIM), F32), unroll=4)

    def prepare(h, carry):
        at = columns(h)
        grown = jnp.exp(cum_col[:, at])
        lead[:, at] = grown
        high, low = split(jnp.transpose(query[:, at].astype(F32) * grown))
        turned_query[h] = jnp.concatenate([high, low], axis=0)
        scaled[:, at] = cot[:, at].astype(F32) * gain_ref[:, at]
        return carry

    lax.fori_loop(0, heads, forward, 0)
    lax.fori_loop(0, heads, prepare, 0)
    pltpu.make_async_copy(totals, totals, total_sem.at[1]).wait()
    totals[...] = jnp.exp(totals[...])
    for part in range(parts):
        given(arrived, 0, part)
        advance(part)
        take_all(before, state, 0, part)

    def finish_out(i, carry):
        squares, inners = carry
        h = lax.rem(spot + plane_size - turn_of(i), plane_size)
        taken(state, 0, h)
        at = columns(h)
        high, low = split(load_state(state, h))
        outer = mul(query[:, at], jnp.concatenate([high, low], axis=1), NN)
        whole = out[:, at] + lead[:, at] * (outer[:, :DIM] + outer[:, DIM:])
        out[:, at] = whole
        return squares + whole * whole, inners + scaled[:, at] * whole

    zero = jnp.zeros((BLOCK, DIM), F32)
    squares, inners = lax.fori_loop(0, heads, finish_out, (zero, zero))
    lanes = lax.broadcasted_iota(jnp.int32, (DIM, DIM), 1)
    packed = jnp.zeros((DIM, DIM), F32)
    for which, sums in enumerate((squares, inners)):
        sums = jnp.sum(sums, axis=1, keepdims=True)
        for i in range(BLOCK // DIM):
            packed = jnp.where(lanes == 4 * which + i, sums[i * DIM : (i + 1) * DIM], packed)
    stat[...] = jnp.transpose(packed)[:8]
    pltpu.make_async_copy(stat, stats.at[place], stat_sem.at[1]).start()

    def share_stat(d, carry):
        peer = lax.rem(place + d, head_count)
        remote(stat, stats.at[place], stat_sem.at[0], stat_sem.at[1], {"head": peer})
        return carry

    lax.fori_loop(1, head_count, share_stat, 0)
    pltpu.make_async_copy(stats, stats, stat_sem.at[1]).wait()
    summed = stats[0]
    for i in range(1, head_count):
        summed = summed + stats[i]
    inverse_rows = lax.rsqrt(summed[:4] / features + EPSILON)
    mean_rows = inverse_rows * summed[4:] / features

    turned = jnp.transpose(jnp.concatenate([inverse_rows, mean_rows] * (DIM // 8), axis=0))

    def to_columns(first):
        return jnp.concatenate(
            [jnp.broadcast_to(turned[:, i : i + 1], (DIM, DIM)) for i in range(first, first + 4)], axis=0
        )

    inverse = to_columns(0)
    mean_term = to_columns(4)

    def make_grad(i, carry):
        h = lax.rem(spot + turn_of(i), plane_size)
        at = columns(h)
        normed = out[:, at] * inverse
        out[:, at] = normed
        g = (inverse * (scaled[:, at] - normed * mean_term)).astype(BF16)
        grad[:, at] = g
        both = mul(turned_query[h], g, NN)
        store_piece(grad_piece, h, both[:DIM] + both[DIM:])
        return h

    def make_and_give(i, carry):
        give_head(grad_piece, grad_arrived, 1, 0, make_grad(i, carry), False)
        return carry

    lax.fori_loop(0, heads - 1, make_and_give, 0)
    make_grad(heads - 1, 0)
    give_head(grad_piece, grad_arrived, 1, 0, spot, True)
    for part in range(1, parts):
        give_all(grad_piece, grad_arrived, 1, part)

    def backward(h, carry):
        at = columns(h)
        d0 = decay0[h]
        d1 = decay1[h]
        keys = key[:, at]
        values = value[:, at]
        g = grad[:, at]
        q = query[:, at]
        w0 = weight0[h]
        w1 = weight1[h]
        att[:, at] = (out[:, at] * gain_ref[:, at]).astype(BF16)
        g0 = (mul(g[:HALF], values[:HALF], NT) * d0).astype(BF16)
        g1 = (mul(g[HALF:], values, NT) * d1).astype(BF16)
        high, low = split(load_state(state, h))
        outer = lead[:, at] * (mul(g, high, NT) + mul(g, low, NT))
        gq[:HALF, at] = (mul(g0, keys[:HALF], NN) + outer[:HALF]).astype(BF16)
        gq[HALF:, at] = (mul(g1, keys, NN) + outer[HALF:]).astype(BF16)
        full_key = mul(g1, q[HALF:], TN)
        full_value = mul(w1, g[HALF:], TN)
        inner_key[:HALF, at] = full_key[:HALF] + mul(g0, q[:HALF], TN)
        inner_key[HALF:, at] = full_key[HALF:]
        inner_value[:HALF, at] = full_value[:HALF] + mul(w0, g[:HALF], TN)
        inner_value[HALF:, at] = full_value[HALF:]
        return carry

    def retreat(part):
        at = part_rows(part)

        def one(turn, running):
            b = seq_count - 1 - turn
            after[b, at] = running
            return grad_arrived[b, at] + totals[b] * running

        lax.fori_loop(0, seq_count, one, jnp.zeros((part_size, DIM), F32), unroll=4)

    lax.fori_loop(0, heads, backward, 0)
    for part in range(parts):
        given(grad_arrived, 1, part)
        retreat(part)
        take_all(after, after_state, 1, part)

    def finish(i, carry):
        h = lax.rem(spot + plane_size - turn_of(i), plane_size)
        taken(after_state, 1, h)
        at = columns(h)
        high, low = split(load_state(after_state, h))
        shrunk = trail[:, at]
        values = value[:, at]
        from_value = mul(values, high, NT) + mul(values, low, NT)
        gk[:, at] = (inner_key[:, at] + shrunk * from_value).astype(BF16)
        from_key = mul(key[:, at], jnp.concatenate([high, low], axis=1), NN)
        gv[:, at] = (
            inner_value[:, at] + shrunk * (from_key[:, :DIM] + from_key[:, DIM:])
        ).astype(BF16)
        return carry

    lax.fori_loop(0, heads, finish, 0)

    some = totals.at[pl.ds(0, seq_count - 1)]
    pltpu.make_async_copy(some, some, total_sem.at[0]).wait()
    some = stats.at[pl.ds(0, head_count - 1)]
    pltpu.make_async_copy(some, some, stat_sem.at[0]).wait()
    for which in range(2):
        for part in range(parts):
            sent(piece, give_send.at[which, part])
            sent(piece, take_send.at[which, part])


def on_device(seq_count, head_count, queries, key_vecs, value_vecs, log_decay, norm_gain, cotangent):
    tokens, width = queries.shape
    heads = width // DIM
    rows = heads * DIM // seq_count
    planes = seq_count // heads
    vmem = pl.BlockSpec(memory_space=pltpu.VMEM)
    hbm = pl.BlockSpec(memory_space=pltpu.HBM)
    narrow = pltpu.VMEM((tokens, width), BF16)
    wide = pltpu.VMEM((tokens, width), F32)
    chunk = pltpu.VMEM((seq_count, rows, DIM), F32)
    line = pltpu.VMEM((seq_count, 1, DIM), F32)
    pair = pltpu.SemaphoreType.DMA((2,))
    square = pltpu.SemaphoreType.DMA((2, PARTS))
    results = pl.pallas_call(
        functools.partial(kernel, PARTS, planes, heads, head_count, heads),
        out_shape=(narrow,) * 4,
        in_specs=[hbm] * 6,
        out_specs=(vmem,) * 4,
        scratch_shapes=[pltpu.VMEM((heads, tokens), F32), pltpu.VMEM((1, width), F32)]
        + [narrow] * 4
        + [
            pltpu.VMEM((heads, tokens), F32),
            wide,
            wide,
            wide,
            pltpu.VMEM((heads, HALF, HALF), F32),
            pltpu.VMEM((heads, HALF, BLOCK), F32),
            pltpu.VMEM((heads, HALF, HALF), BF16),
            pltpu.VMEM((heads, HALF, BLOCK), BF16),
            wide,
            wide,
            pltpu.VMEM((heads, 2 * DIM, tokens), BF16),
            narrow,
            wide,
            wide,
            line,
            line,
        ]
        + [chunk] * 8
        + [pltpu.VMEM((8, DIM), F32), pltpu.VMEM((head_count, 8, DIM), F32)]
        + [pltpu.SemaphoreType.DMA((6,)), pair, pair, square, square, square]
        + [pltpu.SemaphoreType.DMA((2, heads))],
        compiler_params=pltpu.CompilerParams(
            collective_id=0, has_side_effects=True, vmem_limit_bytes=59 * 1024 * 1024
        ),
    )(log_decay.T, norm_gain.reshape(1, width), queries, key_vecs, value_vecs, cotangent)
    return pl.pallas_call(
        store_kernel,
        out_shape=(jax.ShapeDtypeStruct((tokens, width), BF16),) * 4,
        in_specs=[vmem] * 4,
        out_specs=(hbm,) * 4,
        scratch_shapes=[pltpu.SemaphoreType.DMA((4,))],
        compiler_params=pltpu.CompilerParams(vmem_limit_bytes=8 * 1024 * 1024),
    )(*results)


def solution(mesh):
    return jax.shard_map(
        functools.partial(on_device, mesh.shape["seq"], mesh.shape["head"]),
        mesh=mesh,
        in_specs=(
            P("seq", "head"),
            P("seq", "head"),
            P("seq", "head"),
            P("seq", "head"),
            P("head"),
            P("seq", "head"),
        ),
        out_specs=(P("seq", "head"), P("seq", "head"), P("seq", "head"), P("seq", "head")),
        check_vma=False,
    )
```

```python
import functools

import jax
import jax.numpy as jnp
from jax import lax
from jax.experimental import pallas as pl
from jax.experimental.pallas import tpu as pltpu
from jax.sharding import PartitionSpec as P

DIM = 128
BLOCK = 512
HALF = 256
PARTS = 2
EPSILON = 1e-06
F32 = jnp.float32
BF16 = jnp.bfloat16
NN = (((1,), (0,)), ((), ()))
NT = (((1,), (1,)), ((), ()))
TN = (((0,), (0,)), ((), ()))


def mul(a, b, dims):
    return lax.dot_general(a, b, dims, preferred_element_type=F32)


def split(x):
    high = x.astype(BF16)
    return high, (x - high.astype(F32)).astype(BF16)


def store_kernel(*refs):
    sources, targets, sem = refs[:4], refs[4:8], refs[8]
    copies = [
        pltpu.make_async_copy(source, target, sem.at[i])
        for i, (source, target) in enumerate(zip(sources, targets))
    ]
    for copy in copies:
        copy.start()
    for copy in copies:
        copy.wait()


def kernel(
    parts, planes, plane_size, head_count, heads,
    log_hbm, gain_hbm, query_hbm, key_hbm, value_hbm, cot_hbm,
    att, gq, gk, gv,
    log_ref, gain_ref, query, key, value, cot,
    cum_row, cum_col, lead, trail, decay0, decay1, weight0, weight1,
    out, scaled, turned_query, grad, inner_key, inner_value,
    own_total, totals,
    piece, arrived, before, state,
    grad_piece, grad_arrived, after, after_state,
    stat, stats,
    in_sem, total_sem, stat_sem, give_send, give_receive, take_send, take_receive,
):
    me = lax.axis_index("seq")
    plane = me // plane_size
    spot = lax.rem(me, plane_size)
    place = lax.axis_index("head")
    seq_count = planes * plane_size
    rows = piece.shape[1]
    part_size = rows // parts
    features = head_count * heads * DIM

    barrier = pltpu.get_barrier_semaphore()

    def greet_seq(d, carry):
        pl.semaphore_signal(
            barrier, inc=1, device_id={"seq": lax.rem(me + d + seq_count // 2, seq_count)},
            device_id_type=pl.DeviceIdType.MESH,
        )
        return carry

    def greet_head(d, carry):
        pl.semaphore_signal(
            barrier, inc=1, device_id={"head": lax.rem(place + d, head_count)},
            device_id_type=pl.DeviceIdType.MESH,
        )
        return carry

    lax.fori_loop(0, seq_count // 2, greet_seq, 0)
    lax.fori_loop(seq_count // 2 + 1, seq_count, greet_seq, 0)
    lax.fori_loop(1, head_count, greet_head, 0)
    loads = [
        pltpu.make_async_copy(source, target, in_sem.at[i])
        for i, (source, target) in enumerate(
            (
                (log_hbm, log_ref), (key_hbm, key), (value_hbm, value),
                (query_hbm, query), (cot_hbm, cot), (gain_hbm, gain_ref),
            )
        )
    ]
    for load in loads:
        load.start()

    def columns(h):
        return pl.ds(pl.multiple_of(h * DIM, DIM), DIM)

    def turn_of(i):
        return lax.rem(plane_size // 2 + (1 - 2 * lax.rem(place, 2)) * (1 - 2 * lax.rem(i, 2)) * ((i + 1) // 2), plane_size)

    def part_rows(part):
        return pl.ds(part * part_size, part_size)

    def slots(h):
        return pl.ds(pl.multiple_of(h * planes, planes), planes)

    def remote(source, target, send, receive, peer):
        pltpu.make_async_remote_copy(
            src_ref=source, dst_ref=target, send_sem=send, recv_sem=receive,
            device_id=peer, device_id_type=pl.DeviceIdType.MESH,
        ).start()

    def give_head(source, target, which, part, h, own):
        at = part_rows(part)
        for d in (2, 1, 3, 0):
            p = lax.rem(plane + d * (1 + 2 * lax.rem(place, 2)), planes)
            if own and d == 0:
                pltpu.make_async_copy(
                    source.at[h * planes + p, at], target.at[me, at], give_receive.at[which, part]
                ).start()
            else:
                remote(
                    source.at[h * planes + p, at], target.at[me, at],
                    give_send.at[which, part], give_receive.at[which, part],
                    {"seq": p * plane_size + h},
                )

    def give_all(source, target, which, part):
        def one(i, carry):
            give_head(source, target, which, part, lax.rem(spot + turn_of(i), plane_size), False)
            return carry

        lax.fori_loop(0, plane_size - 1, one, 0, unroll=True)
        give_head(source, target, which, part, spot, True)

    def take_all(source, target, which, part):
        at = part_rows(part)
        slot = spot * planes + plane

        def one_spot(z, own):
            for d in (2, 1, 3, 0):
                p = lax.rem(plane + d * (1 + 2 * lax.rem(place, 2)), planes)
                b = p * plane_size + z
                if own and d == 0:
                    pltpu.make_async_copy(
                        source.at[b, at], target.at[slot, at], take_receive.at[which, spot]
                    ).start()
                else:
                    remote(
                        source.at[b, at], target.at[slot, at],
                        take_send.at[which, part], take_receive.at[which, spot], {"seq": b},
                    )

        def one(i, carry):
            one_spot(lax.rem(spot + turn_of(i), plane_size), False)
            return carry

        lax.fori_loop(0, plane_size - 1, one, 0, unroll=True)
        one_spot(spot, True)

    def given(target, which, part):
        some = target.at[:, part_rows(part)]
        pltpu.make_async_copy(some, some, give_receive.at[which, part]).wait()

    def taken(target, which, h):
        some = target.at[slots(h)]
        pltpu.make_async_copy(some, some, take_receive.at[which, h]).wait()

    def sent(target, send):
        some = target.at[pl.ds(0, seq_count - 1), part_rows(0)]
        pltpu.make_async_copy(some, some, send).wait()

    def store_piece(target, h, result):
        target[slots(h)] = result.reshape(planes, rows, DIM)

    def load_state(source, h):
        return source[slots(h)].reshape(DIM, DIM)

    lower = lax.broadcasted_iota(jnp.int32, (BLOCK, BLOCK), 0) >= lax.broadcasted_iota(
        jnp.int32, (BLOCK, BLOCK), 1
    )
    lower = lower.astype(F32).astype(BF16)
    loads[0].wait()
    logs = log_ref[...]
    high, low = split(logs)
    rest = (logs - high.astype(F32) - low.astype(F32)).astype(BF16)
    terms = mul(jnp.concatenate([high, low, rest], axis=0), lower, NT)
    cumulative = terms[:heads] + (terms[heads : 2 * heads] + terms[2 * heads :])
    cum_row[...] = cumulative
    turned = jnp.transpose(jnp.concatenate([cumulative] * (DIM // heads), axis=0))
    for h in range(heads):
        spread = jnp.broadcast_to(turned[:, h : h + 1], (BLOCK, DIM))
        cum_col[:, h * DIM : (h + 1) * DIM] = spread
        total = spread[BLOCK - 1 :, :]
        trail[:, h * DIM : (h + 1) * DIM] = jnp.exp(total - spread)
        for p in range(planes):
            own_total[h * planes + p] = total

    loads[1].wait()
    loads[2].wait()

    def make_piece(h, carry):
        at = columns(h)
        high, low = split(key[:, at].astype(F32) * trail[:, at])
        both = value[:, at]
        store_piece(piece, h, mul(high, both, TN) + mul(low, both, TN))
        return carry

    def head_at(i):
        return lax.rem(spot + turn_of(i), plane_size)

    def make_and_give_piece(i, carry):
        give_head(piece, arrived, 0, 0, head_at(i), False)
        make_piece(head_at(i + 1), carry)
        return carry

    make_piece(head_at(0), 0)
    pl.semaphore_wait(barrier, seq_count + head_count - 2)
    lax.fori_loop(0, heads - 1, make_and_give_piece, 0)
    give_head(piece, arrived, 0, 0, spot, True)

    pltpu.make_async_copy(
        own_total.at[spot * planes + plane], totals.at[me], total_sem.at[1]
    ).start()

    def share_total(d, carry):
        peer = lax.rem(me + d, seq_count)
        slot = lax.rem(peer, plane_size) * planes + peer // plane_size
        remote(own_total.at[slot], totals.at[me], total_sem.at[0], total_sem.at[1], {"seq": peer})
        return carry

    lax.fori_loop(1, seq_count, share_total, 0)
    for part in range(1, parts):
        give_all(piece, arrived, 0, part)

    for load in loads[3:]:
        load.wait()
    causal = lax.broadcasted_iota(jnp.int32, (HALF, HALF), 0) >= lax.broadcasted_iota(
        jnp.int32, (HALF, HALF), 1
    )

    def forward(h, carry):
        at = columns(h)
        row = cum_row[pl.ds(h, 1), :]
        col = cum_col[:, at]
        top = jnp.concatenate([col[:HALF]] * 2, axis=1)
        low = jnp.concatenate([col[HALF:]] * 2, axis=1)
        left, right = row[:, :HALF], row[:, HALF:]
        masked = -1e30
        d0 = jnp.exp(jnp.where(causal, top - left, masked))
        d1 = jnp.concatenate(
            [jnp.exp(low - left), jnp.exp(jnp.where(causal, low - right, masked))], axis=1
        )
        decay0[h] = d0
        decay1[h] = d1
        keys = key[:, at]
        values = value[:, at]
        w0 = (mul(query[:HALF, at], keys[:HALF], NT) * d0).astype(BF16)
        w1 = (mul(query[HALF:, at], keys, NT) * d1).astype(BF16)
        weight0[h] = w0
        weight1[h] = w1
        out[:HALF, at] = mul(w0, values[:HALF], NN)
        out[HALF:, at] = mul(w1, values, NN)
        return carry

    def advance(part):
        at = part_rows(part)

        def one(b, running):
            before[b, at] = running
            return totals[b] * running + arrived[b, at]

        lax.fori_loop(0, seq_count, one, jnp.zeros((part_size, DIM), F32), unroll=8)

    def prepare(h, carry):
        at = columns(h)
        grown = jnp.exp(cum_col[:, at])
        lead[:, at] = grown
        high, low = split(jnp.transpose(query[:, at].astype(F32) * grown))
        turned_query[h] = jnp.concatenate([high, low], axis=0)
        scaled[:, at] = cot[:, at].astype(F32) * gain_ref[:, at]
        return carry

    lax.fori_loop(0, heads, forward, 0)
    lax.fori_loop(0, heads, prepare, 0)
    pltpu.make_async_copy(totals, totals, total_sem.at[1]).wait()
    totals[...] = jnp.exp(totals[...])
    for part in range(parts):
        given(arrived, 0, part)
        advance(part)
        take_all(before, state, 0, part)

    def finish_out(i, carry):
        squares, inners = carry
        h = lax.rem(spot + plane_size - turn_of(i), plane_size)
        taken(state, 0, h)
        at = columns(h)
        high, low = split(load_state(state, h))
        outer = mul(query[:, at], jnp.concatenate([high, low], axis=1), NN)
        whole = out[:, at] + lead[:, at] * (outer[:, :DIM] + outer[:, DIM:])
        out[:, at] = whole
        return squares + whole * whole, inners + scaled[:, at] * whole

    zero = jnp.zeros((BLOCK, DIM), F32)
    squares, inners = lax.fori_loop(0, heads, finish_out, (zero, zero))
    lanes = lax.broadcasted_iota(jnp.int32, (DIM, DIM), 1)
    packed = jnp.zeros((DIM, DIM), F32)
    for which, sums in enumerate((squares, inners)):
        sums = jnp.sum(sums, axis=1, keepdims=True)
        for i in range(BLOCK // DIM):
            packed = jnp.where(lanes == 4 * which + i, sums[i * DIM : (i + 1) * DIM], packed)
    stat[...] = jnp.transpose(packed)[:8]
    pltpu.make_async_copy(stat, stats.at[place], stat_sem.at[1]).start()

    def share_stat(i, carry):
        d = head_count // 2 + (1 - 2 * lax.rem(i, 2)) * ((i + 1) // 2)
        peer = lax.rem(place + d, head_count)
        remote(stat, stats.at[place], stat_sem.at[0], stat_sem.at[1], {"head": peer})
        return carry

    lax.fori_loop(0, head_count - 1, share_stat, 0, unroll=True)
    pltpu.make_async_copy(stats, stats, stat_sem.at[1]).wait()
    summed = stats[0]
    for i in range(1, head_count):
        summed = summed + stats[i]
    inverse_rows = lax.rsqrt(summed[:4] / features + EPSILON)
    mean_rows = inverse_rows * summed[4:] / features

    turned = jnp.transpose(jnp.concatenate([inverse_rows, mean_rows] * (DIM // 8), axis=0))

    def to_columns(first):
        return jnp.concatenate(
            [jnp.broadcast_to(turned[:, i : i + 1], (DIM, DIM)) for i in range(first, first + 4)], axis=0
        )

    inverse = to_columns(0)
    mean_term = to_columns(4)

    def make_grad(i, carry):
        h = lax.rem(spot + turn_of(i), plane_size)
        at = columns(h)
        normed = out[:, at] * inverse
        out[:, at] = normed
        g = (inverse * (scaled[:, at] - normed * mean_term)).astype(BF16)
        grad[:, at] = g
        both = mul(turned_query[h], g, NN)
        store_piece(grad_piece, h, both[:DIM] + both[DIM:])
        return h

    def make_and_give(i, carry):
        give_head(grad_piece, grad_arrived, 1, 0, make_grad(i, carry), False)
        return carry

    lax.fori_loop(0, heads - 1, make_and_give, 0)
    make_grad(heads - 1, 0)
    give_head(grad_piece, grad_arrived, 1, 0, spot, True)
    for part in range(1, parts):
        give_all(grad_piece, grad_arrived, 1, part)

    def backward(h, carry):
        at = columns(h)
        d0 = decay0[h]
        d1 = decay1[h]
        keys = key[:, at]
        values = value[:, at]
        g = grad[:, at]
        q = query[:, at]
        w0 = weight0[h]
        w1 = weight1[h]
        att[:, at] = (out[:, at] * gain_ref[:, at]).astype(BF16)
        g0 = (mul(g[:HALF], values[:HALF], NT) * d0).astype(BF16)
        g1 = (mul(g[HALF:], values, NT) * d1).astype(BF16)
        high, low = split(load_state(state, h))
        outer = lead[:, at] * (mul(g, high, NT) + mul(g, low, NT))
        gq[:HALF, at] = (mul(g0, keys[:HALF], NN) + outer[:HALF]).astype(BF16)
        gq[HALF:, at] = (mul(g1, keys, NN) + outer[HALF:]).astype(BF16)
        full_key = mul(g1, q[HALF:], TN)
        full_value = mul(w1, g[HALF:], TN)
        inner_key[:HALF, at] = full_key[:HALF] + mul(g0, q[:HALF], TN)
        inner_key[HALF:, at] = full_key[HALF:]
        inner_value[:HALF, at] = full_value[:HALF] + mul(w0, g[:HALF], TN)
        inner_value[HALF:, at] = full_value[HALF:]
        return carry

    def retreat(part):
        at = part_rows(part)

        def one(turn, running):
            b = seq_count - 1 - turn
            after[b, at] = running
            return grad_arrived[b, at] + totals[b] * running

        lax.fori_loop(0, seq_count, one, jnp.zeros((part_size, DIM), F32), unroll=8)

    lax.fori_loop(0, heads, backward, 0)
    for part in range(parts):
        given(grad_arrived, 1, part)
        retreat(part)
        take_all(after, after_state, 1, part)

    def finish(i, carry):
        h = lax.rem(spot + plane_size - turn_of(i), plane_size)
        taken(after_state, 1, h)
        at = columns(h)
        high, low = split(load_state(after_state, h))
        shrunk = trail[:, at]
        values = value[:, at]
        from_value = mul(values, high, NT) + mul(values, low, NT)
        gk[:, at] = (inner_key[:, at] + shrunk * from_value).astype(BF16)
        from_key = mul(key[:, at], jnp.concatenate([high, low], axis=1), NN)
        gv[:, at] = (
            inner_value[:, at] + shrunk * (from_key[:, :DIM] + from_key[:, DIM:])
        ).astype(BF16)
        return carry

    lax.fori_loop(0, heads, finish, 0)

    some = totals.at[pl.ds(0, seq_count - 1)]
    pltpu.make_async_copy(some, some, total_sem.at[0]).wait()
    some = stats.at[pl.ds(0, head_count - 1)]
    pltpu.make_async_copy(some, some, stat_sem.at[0]).wait()
    for which in range(2):
        for part in range(parts):
            sent(piece, give_send.at[which, part])
            sent(piece, take_send.at[which, part])


def on_device(seq_count, head_count, queries, key_vecs, value_vecs, log_decay, norm_gain, cotangent):
    tokens, width = queries.shape
    heads = width // DIM
    rows = heads * DIM // seq_count
    planes = seq_count // heads
    vmem = pl.BlockSpec(memory_space=pltpu.VMEM)
    hbm = pl.BlockSpec(memory_space=pltpu.HBM)
    narrow = pltpu.VMEM((tokens, width), BF16)
    wide = pltpu.VMEM((tokens, width), F32)
    chunk = pltpu.VMEM((seq_count, rows, DIM), F32)
    line = pltpu.VMEM((seq_count, 1, DIM), F32)
    pair = pltpu.SemaphoreType.DMA((2,))
    square = pltpu.SemaphoreType.DMA((2, PARTS))
    results = pl.pallas_call(
        functools.partial(kernel, PARTS, planes, heads, head_count, heads),
        out_shape=(narrow,) * 4,
        in_specs=[hbm] * 6,
        out_specs=(vmem,) * 4,
        scratch_shapes=[pltpu.VMEM((heads, tokens), F32), pltpu.VMEM((1, width), F32)]
        + [narrow] * 4
        + [
            pltpu.VMEM((heads, tokens), F32),
            wide,
            wide,
            wide,
            pltpu.VMEM((heads, HALF, HALF), F32),
            pltpu.VMEM((heads, HALF, BLOCK), F32),
            pltpu.VMEM((heads, HALF, HALF), BF16),
            pltpu.VMEM((heads, HALF, BLOCK), BF16),
            wide,
            wide,
            pltpu.VMEM((heads, 2 * DIM, tokens), BF16),
            narrow,
            wide,
            wide,
            line,
            line,
        ]
        + [chunk] * 8
        + [pltpu.VMEM((8, DIM), F32), pltpu.VMEM((head_count, 8, DIM), F32)]
        + [pltpu.SemaphoreType.DMA((6,)), pair, pair, square, square, square]
        + [pltpu.SemaphoreType.DMA((2, heads))],
        compiler_params=pltpu.CompilerParams(
            collective_id=0, has_side_effects=True, vmem_limit_bytes=59 * 1024 * 1024
        ),
    )(log_decay.T, norm_gain.reshape(1, width), queries, key_vecs, value_vecs, cotangent)
    return pl.pallas_call(
        store_kernel,
        out_shape=(jax.ShapeDtypeStruct((tokens, width), BF16),) * 4,
        in_specs=[vmem] * 4,
        out_specs=(hbm,) * 4,
        scratch_shapes=[pltpu.SemaphoreType.DMA((4,))],
        compiler_params=pltpu.CompilerParams(vmem_limit_bytes=8 * 1024 * 1024),
    )(*results)


def solution(mesh):
    return jax.shard_map(
        functools.partial(on_device, mesh.shape["seq"], mesh.shape["head"]),
        mesh=mesh,
        in_specs=(
            P("seq", "head"),
            P("seq", "head"),
            P("seq", "head"),
            P("seq", "head"),
            P("head"),
            P("seq", "head"),
        ),
        out_specs=(P("seq", "head"), P("seq", "head"), P("seq", "head"), P("seq", "head")),
        check_vma=False,
    )
```
